32 devices in a mesh: atoms: 8 (over z, y), waves: 4 (over x, core).
Axes of the slice: x: 2, y: 2, z: 4, core: 2. Of those that a mesh axis runs over, the one named last changes fastest.
Arguments:
- features: bfloat16 [2048, 512], P('atoms'), may hold values from -6 to 6
- positions: int32 [3, 2048], P(None, 'atoms'), may hold values from 0 to 65535
- neighbours: int32 [16, 12], P('atoms'), may hold values from 0 to 15, as said below
- wavevectors: int32 [3, 4096], P(None, 'waves'), may hold values from -16 to 16
- radial_width: float32 [8], P('waves'), may hold values from 0.05 to 0.3
- short_weight: bfloat16 [8, 512, 512], P('waves'), may hold values from -0.09375 to 0.09375
- latent_weight: bfloat16 [512, 256], replicated, may hold values from -0.25 to 0.25
- mix_weight: float32 [256, 256], replicated, may hold values from -0.375 to 0.375
- filter_rate: float32 [256], replicated, may hold values from 0.0005 to 0.02
- out_weight: bfloat16 [256, 512], replicated, may hold values from -0.375 to 0.375
Outputs:
- message: bfloat16 [2048, 512], P('atoms', 'waves')
The draws below stay inside these ranges and needn't reach their ends.
Inputs may be any that keep to these rules, and one draw needn't show every extreme that they name: `neighbours`: row b holds 12 different block numbers, each within 7 blocks of b counted cyclically over the 16 blocks; b itself may appear.
All inputs are finite; a program needn't handle non-finite values.
Results may differ from the reference program's by a relative error of at most 0.012.
Values may be sent and summed in bfloat16 or wider, within the bound.
A program may use at most 64 MiB of HBM per device.

```python
import math
import jax
import jax.numpy as jnp
from jax import lax

C = 512
LAT = 256
K = 4096
RADIAL = 8
BLOCK = 128
NBR = 12
REACH = 7
NBLOCKS = 16
NATOMS = 2048
N_WAVES = 4


def draw_neighbours(key, part):
    pop_key, pick_key = jax.random.split(jax.random.fold_in(key, 11))
    span = 2 * REACH + 1
    popularity = jax.random.randint(pop_key, (NBLOCKS,), 0, 4096)
    jitter = jax.random.randint(pick_key, (NBLOCKS, span), 0, 1024)
    shifts = jnp.arange(span, dtype=jnp.int32) - REACH
    block_ids = jnp.arange(NBLOCKS, dtype=jnp.int32)
    target = jnp.mod(block_ids[:, None] + shifts[None, :], NBLOCKS)
    scores = (jitter + popularity[target]) * 32 + (shifts[None, :] + REACH)
    _, picked = lax.top_k(-scores, NBR)
    return jnp.take_along_axis(target, picked, axis=1).astype(jnp.int32)


def with_ends(entries, stream_key, smallest, high):
    place = [jax.random.randint(jax.random.fold_in(stream_key, axis), (), 0, length) for axis, length in enumerate(entries.shape)]
    widest = entries.shape.index(max(entries.shape))
    beside = place[:widest] + [(place[widest] + 1) % entries.shape[widest]] + place[widest + 1:]
    return entries.at[tuple(place)].set(smallest).at[tuple(beside)].set(high)


def shard_levels(key, shape, shards, least, top_value):
    def one(position, shards_of):
        heights = jax.random.uniform(jax.random.fold_in(jax.random.fold_in(key, 6), position), (shards_of,), jnp.float32, least / len(shards), top_value / len(shards))
        return jnp.repeat(jnp.exp(heights), shape[position] // shards_of).reshape((-1,) + (1,) * (len(shape) - position - 1))

    level = one(*shards[0])
    for cut in shards[1:]:
        level = level * one(*cut)
    return level


def noise(stream_key, dims, deviation, reach, pieces=(), kind=jnp.bfloat16):
    values = jax.random.normal(stream_key, dims, jnp.float32) * deviation
    if len(pieces) > 0:
        values = shard_levels(stream_key, dims, pieces, -0.22, 0.18) * values
    return jnp.clip(values, min=-reach, max=reach).astype(kind)


def setup_inputs(seed: int = 0) -> dict:
    key_list = jax.random.split(jax.random.key(seed), 11)
    features = noise(key_list[0], (NATOMS, C), 1.0, 6.0, ((0, 8),))
    positions = with_ends(jax.random.randint(key_list[1], (3, NATOMS), 0, 65536), jax.random.fold_in(key_list[1], 1), 0, 65535).astype(jnp.int32)
    neighbours = draw_neighbours(jax.random.fold_in(key_list[10], 71), 0)
    wavevectors = with_ends(jax.random.randint(key_list[3], (3, K), -16, 17), jax.random.fold_in(key_list[3], 1), -16, 16).astype(jnp.int32)
    radial_width = jnp.clip(jnp.exp(math.log(0.3) - 1.7917595 * jax.random.uniform(key_list[4], (RADIAL,), jnp.float32) ** shard_levels(key_list[4], (RADIAL,), ((0, 4),), -0.2, 0.2)), 0.05, 0.3)
    short_weight = noise(key_list[5], (RADIAL, C, C), (RADIAL * C) ** -0.5, 0.09375, ((0, 4),))
    latent_weight = noise(key_list[6], (C, LAT), C ** -0.5, 0.25)
    mix_weight = noise(key_list[7], (LAT, LAT), LAT ** -0.5, 0.375, (), jnp.float32)
    filter_rate = jnp.clip(jnp.exp(jax.random.uniform(key_list[8], (LAT,), jnp.float32, math.log(0.0005), math.log(0.02))), 0.0005, 0.02)
    out_weight = noise(key_list[9], (LAT, C), LAT ** -0.5, 0.375)
    return dict(features=features, positions=positions, neighbours=neighbours, wavevectors=wavevectors, radial_width=radial_width, short_weight=short_weight, latent_weight=latent_weight, mix_weight=mix_weight, filter_rate=filter_rate, out_weight=out_weight)


cutoff = 0.5

def kernels(own_pos, near_pos, centers, radial_width):
    offsets = own_pos[:, None, :, None] - near_pos[:, :, None, :]
    offsets = jnp.mod(offsets, 65536)
    offsets = jnp.where(offsets >= 32768, offsets - 65536, offsets)
    coords = offsets.astype(jnp.float32) * (1.0 / 65536.0)
    dist_sq = lax.optimization_barrier(jnp.sum(coords * coords, axis=0))
    distance = jnp.sqrt(dist_sq)
    smooth = jnp.where(dist_sq < cutoff * cutoff, jnp.square(1.0 - dist_sq / (cutoff * cutoff)), 0.0)
    shaped = (distance[None] - centers[:, None, None, None]) / radial_width[:, None, None, None]
    norm_scale = 1.0 / math.sqrt(NBR * BLOCK)
    return (jnp.exp(-jnp.square(shaped)) * smooth[None] * norm_scale).astype(jnp.bfloat16)

def phases_of(wavevectors, spots):
    phase_turn = wavevectors[0][:, None] * spots[0][None, :] + wavevectors[1][:, None] * spots[1][None, :] + wavevectors[2][:, None] * spots[2][None, :]
    phase_turn = jnp.mod(phase_turn, 65536)
    angles = phase_turn.astype(jnp.float32) * (2.0 * math.pi / 65536.0)
    return jnp.concatenate([jnp.cos(angles), jnp.sin(angles)], axis=0).astype(jnp.bfloat16)

def filter_gain(wavevectors, filter_rate):
    lengths = lax.optimization_barrier(jnp.sum(wavevectors * wavevectors, axis=0)).astype(jnp.float32)
    return jnp.exp(-lengths[:, None] * filter_rate[None, :])

def reference(features, positions, neighbours, wavevectors, radial_width, short_weight, latent_weight, mix_weight, filter_rate, out_weight):
    block_count = neighbours.shape[0]
    feat_blocks = features.reshape(block_count, BLOCK, C)
    pos_blocks = positions.reshape(3, block_count, BLOCK)
    centers = cutoff * jnp.arange(RADIAL).astype(jnp.float32) / (RADIAL - 1)
    flat_weight = short_weight.reshape(RADIAL * C, C)

    def short_block(block_index):
        near_blocks = neighbours[block_index]
        near_feat = feat_blocks[near_blocks]
        near_pos = pos_blocks[:, near_blocks]
        weights = kernels(pos_blocks[:, block_index], near_pos, centers, radial_width)
        gathered = jnp.einsum('rjia,jac->irc', weights.astype(jnp.float32), near_feat.astype(jnp.float32))
        gathered = gathered.astype(jnp.bfloat16).reshape(BLOCK, RADIAL * C)
        return jnp.dot(gathered, flat_weight, preferred_element_type=jnp.float32)
    block_ids = jnp.arange(block_count, dtype=jnp.int32)
    short_range = lax.map(short_block, block_ids).reshape(block_count * BLOCK, C)
    latent = jnp.dot(features, latent_weight, preferred_element_type=jnp.float32).astype(jnp.bfloat16)
    lat_blocks = latent.reshape(block_count, BLOCK, LAT)

    def add_factor(running, block_index):
        phases = phases_of(wavevectors, pos_blocks[:, block_index])
        return (running + jnp.dot(phases, lat_blocks[block_index], preferred_element_type=jnp.float32), None)
    factors, _ = lax.scan(add_factor, jnp.zeros((2 * K, LAT), jnp.float32), block_ids)
    gain = filter_gain(wavevectors, filter_rate)
    gain = jnp.concatenate([gain, gain], axis=0)
    norm_scale = 1.0 / math.sqrt(block_count * BLOCK)
    mixed = jnp.dot(factors, mix_weight, precision=lax.Precision.HIGHEST)
    filtered = (gain * mixed * norm_scale).astype(jnp.bfloat16)
    group_size = K // N_WAVES

    def long_block(block_index):
        phases = phases_of(wavevectors, pos_blocks[:, block_index])
        running = jnp.zeros((BLOCK, C), jnp.float32)
        for wave_group in range(N_WAVES):
            low = wave_group * group_size
            group_rows = jnp.concatenate([phases[low:low + group_size], phases[K + low:K + low + group_size]], axis=0)
            group_filter = jnp.concatenate([filtered[low:low + group_size], filtered[K + low:K + low + group_size]], axis=0)
            summed = lax.dot_general(group_rows, group_filter, (((0,), (0,)), ((), ())), preferred_element_type=jnp.float32)
            summed = (summed * (1.0 / math.sqrt(K))).astype(jnp.bfloat16)
            running = running + jnp.dot(summed, out_weight, preferred_element_type=jnp.float32)
        return running
    long_range = lax.map(long_block, block_ids).reshape(block_count * BLOCK, C)
    return (short_range + long_range).astype(jnp.bfloat16)
```

```python
import functools
import math

import jax
import jax.numpy as jnp
from jax import lax
from jax.experimental import pallas as pl
from jax.experimental.pallas import tpu as pltpu
from jax.sharding import PartitionSpec as P

K = 4096
RADIAL = 8
BLOCK = 128
NBR = 12
REACH = 7


cutoff = 0.5


def shifted(value, axis, steps):
    count = lax.axis_size(axis)
    pairs = [(source, (source + steps) % count) for source in range(count)]
    return lax.ppermute(value, axis, pairs)


def kernels(own_pos, near_pos, centers, radial_width):
    offsets = own_pos[:, None, :, None] - near_pos[:, :, None, :]
    offsets = jnp.mod(offsets, 65536)
    offsets = jnp.where(offsets >= 32768, offsets - 65536, offsets)
    coords = offsets.astype(jnp.float32) * (1.0 / 65536.0)
    dist_sq = jnp.sum(coords * coords, axis=0)
    distance = jnp.sqrt(dist_sq)
    smooth = jnp.where(
        dist_sq < cutoff * cutoff, jnp.square(1.0 - dist_sq / (cutoff * cutoff)), 0.0
    )
    shaped = (distance[None] - centers[:, None, None, None]) / radial_width[:, None, None, None]
    norm_scale = 1.0 / math.sqrt(NBR * BLOCK)
    return (jnp.exp(-jnp.square(shaped)) * smooth[None] * norm_scale).astype(jnp.bfloat16)


def phases_of(wavevectors, spots):
    phase_turn = (
        wavevectors[0][:, None] * spots[0][None, :]
        + wavevectors[1][:, None] * spots[1][None, :]
        + wavevectors[2][:, None] * spots[2][None, :]
    )
    phase_turn = jnp.mod(phase_turn, 65536)
    angles = phase_turn.astype(jnp.float32) * (2.0 * math.pi / 65536.0)
    return jnp.concatenate([jnp.cos(angles), jnp.sin(angles)], axis=0).astype(jnp.bfloat16)


def filter_gain(wavevectors, filter_rate):
    lengths = jnp.sum(wavevectors * wavevectors, axis=0).astype(jnp.float32)
    return jnp.exp(-lengths[:, None] * filter_rate[None, :])


def local(
    features,
    positions,
    neighbours,
    wavevectors,
    radial_width,
    short_weight,
    latent_weight,
    mix_weight,
    filter_rate,
    out_weight,
):
    row_count = features.shape[0]
    channels = features.shape[1]
    blocks_here = row_count // BLOCK
    atom_devices = lax.axis_size("atoms")
    total_blocks = blocks_here * atom_devices
    reach_hops = -(-REACH // blocks_here)
    window_feat = []
    window_pos = []
    for offset in range(-reach_hops, reach_hops + 1):
        if offset == 0:
            arrived = (features, positions)
        else:
            arrived = shifted((features, positions), "atoms", -offset)
        window_feat.append(arrived[0])
        window_pos.append(arrived[1])
    window_feat = jnp.concatenate(window_feat, axis=0).reshape(-1, BLOCK, channels)
    window_pos = jnp.concatenate(window_pos, axis=1).reshape(3, -1, BLOCK)
    first_block = lax.axis_index("atoms") * blocks_here - reach_hops * blocks_here
    local_near = jnp.mod(neighbours - first_block, total_blocks)
    own_pos = positions.reshape(3, blocks_here, BLOCK)
    local_kernels = radial_width.shape[0]
    kernel_ids = lax.axis_index("waves") * local_kernels + jnp.arange(
        local_kernels, dtype=jnp.int32
    )
    centers = cutoff * kernel_ids.astype(jnp.float32) / (RADIAL - 1)
    flat_weight = short_weight.reshape(local_kernels * channels, channels)

    def short_block(block_index):
        near_blocks = local_near[block_index]
        near_feat = window_feat[near_blocks]
        near_pos = window_pos[:, near_blocks]
        weights = kernels(own_pos[:, block_index], near_pos, centers, radial_width)
        gathered = jnp.einsum(
            "rjia,jac->irc", weights, near_feat, preferred_element_type=jnp.float32
        )
        gathered = gathered.astype(jnp.bfloat16).reshape(BLOCK, local_kernels * channels)
        return jnp.dot(gathered, flat_weight, preferred_element_type=jnp.float32)

    short_range = lax.map(short_block, jnp.arange(blocks_here, dtype=jnp.int32)).reshape(
        row_count, channels
    )
    latent = jnp.dot(features, latent_weight, preferred_element_type=jnp.float32).astype(
        jnp.bfloat16
    )
    phases = phases_of(wavevectors, positions)
    partial_factors = jnp.dot(phases, latent, preferred_element_type=jnp.float32)
    gain = filter_gain(wavevectors, filter_rate)
    gain = jnp.concatenate([gain, gain], axis=0)
    norm_scale = 1.0 / math.sqrt(row_count * atom_devices)
    factors = lax.psum(partial_factors, "atoms")
    mixed = jnp.dot(factors, mix_weight, precision=lax.Precision.HIGHEST)
    filtered = (gain * mixed * norm_scale).astype(jnp.bfloat16)
    summed = lax.dot_general(
        phases, filtered, (((0,), (0,)), ((), ())), preferred_element_type=jnp.float32
    )
    summed = (summed * (1.0 / math.sqrt(K))).astype(jnp.bfloat16)
    long_range = jnp.dot(summed, out_weight, preferred_element_type=jnp.float32)
    combined = lax.psum_scatter(
        (short_range + long_range).astype(jnp.bfloat16), "waves", scatter_dimension=1, tiled=True
    )
    return combined


MESH = pl.DeviceIdType.MESH
SINE = (6.28318516, -41.34165503, 81.60100405, -76.5497817, 39.53670129)


def sine_of_turn(quarter):
    square = quarter * quarter
    total = SINE[-1] * square + SINE[-2]
    for factor in SINE[-3::-1]:
        total = total * square + factor
    return total * quarter


def cos_sin(turn):
    turn = turn * (1.0 / 65536.0)
    turn = turn - jnp.floor(turn + 0.5)
    shifted_turn = turn - 0.25
    shifted_turn = jnp.where(shifted_turn < -0.5, shifted_turn + 1.0, shifted_turn)
    return (
        sine_of_turn(0.25 - jnp.abs(turn)).astype(jnp.bfloat16),
        sine_of_turn(0.25 - jnp.abs(shifted_turn)).astype(jnp.bfloat16),
    )


def columns_of(rows):
    padded = jnp.concatenate([rows, jnp.zeros((5, rows.shape[1]), jnp.float32)], axis=0)
    turned = padded.T
    return [turned[:, axis : axis + 1] for axis in range(3)]


def rows_of(rows):
    return [rows[axis : axis + 1, :] for axis in range(3)]


def turns(first, second):
    return first[0] * second[0] + first[1] * second[1] + first[2] * second[2]


def fused_kernel(
    n,
    groups,
    feat_ref,
    pos_ref,
    nbr_ref,
    wave_ref,
    width_ref,
    short_ref,
    latw_ref,
    mix_ref,
    rate_ref,
    outw_ref,
    out_ref,
    feat_buf,
    pos_buf,
    fused_w,
    factors,
    gathered,
    phase_buf,
    filt_buf,
    message,
    summed,
    send_buf,
    recv_buf,
    own_sem,
    feat_send,
    feat_recv,
    pos_send,
    pos_recv,
    fwd_send,
    fwd_recv,
    filt_send,
    filt_recv,
    msg_send,
    msg_recv,
):
    me = lax.axis_index("atoms")
    group = lax.axis_index("waves")
    core = lax.rem(group, 2)
    partner = group + 1 - 2 * core
    half, channels = feat_ref.shape[1], feat_ref.shape[2]
    rows = 2 * half
    blocks_here = rows // BLOCK
    local_kernels = short_ref.shape[0]
    waves_each = wave_ref.shape[1] // n

    def peer(step):
        return lax.rem(me + step, n)

    def source(step):
        return lax.rem(me + n - step, n)

    def feat_copy(step):
        return pltpu.make_async_remote_copy(
            src_ref=feat_ref.at[core],
            dst_ref=feat_buf.at[me, core],
            send_sem=feat_send.at[step],
            recv_sem=feat_recv.at[step],
            device_id={"atoms": peer(step)},
            device_id_type=MESH,
        )

    def pos_copy(step):
        return pltpu.make_async_remote_copy(
            src_ref=pos_ref,
            dst_ref=pos_buf.at[me],
            send_sem=pos_send.at[step],
            recv_sem=pos_recv.at[step],
            device_id={"atoms": peer(step)},
            device_id_type=MESH,
        )

    def forward_copy(step):
        return pltpu.make_async_remote_copy(
            src_ref=feat_buf.at[source(step), core],
            dst_ref=feat_buf.at[source(step), core],
            send_sem=fwd_send.at[step],
            recv_sem=fwd_recv.at[step],
            device_id={"waves": partner},
            device_id_type=MESH,
        )

    def filt_copy(step):
        return pltpu.make_async_remote_copy(
            src_ref=filt_buf.at[me],
            dst_ref=filt_buf.at[me],
            send_sem=filt_send.at[step],
            recv_sem=filt_recv.at[step],
            device_id={"atoms": peer(step)},
            device_id_type=MESH,
        )

    def msg_copy(step):
        target = lax.rem(group + step, groups)
        return pltpu.make_async_remote_copy(
            src_ref=send_buf.at[target],
            dst_ref=recv_buf.at[step],
            send_sem=msg_send.at[step],
            recv_sem=msg_recv.at[step],
            device_id={"waves": target},
            device_id_type=MESH,
        )

    own_feat = pltpu.make_async_copy(feat_ref, feat_buf.at[me], own_sem.at[0])
    own_pos = pltpu.make_async_copy(pos_ref, pos_buf.at[me], own_sem.at[1])
    own_feat.start()
    own_pos.start()

    barrier = pltpu.get_barrier_semaphore()
    for step in range(1, n):
        pl.semaphore_signal(barrier, inc=1, device_id={"atoms": peer(step)}, device_id_type=MESH)
    for step in range(1, groups):
        pl.semaphore_signal(
            barrier,
            inc=1,
            device_id={"waves": lax.rem(group + step, groups)},
            device_id_type=MESH,
        )
    pl.semaphore_wait(barrier, n - 1 + groups - 1)

    for step in range(1, n):
        pos_copy(step).start()
        feat_copy(step).start()

    fused_w[...] = jnp.dot(
        latw_ref[...].astype(jnp.float32),
        mix_ref[...],
        precision=lax.Precision.HIGHEST,
        preferred_element_type=jnp.float32,
    ).astype(jnp.bfloat16)
    spots = columns_of(pos_ref[...].astype(jnp.float32))

    def phase_step(which, carry):
        begin = pl.multiple_of(which * waves_each, waves_each)
        waves = rows_of(wave_ref[:, pl.ds(begin, waves_each)].astype(jnp.float32))
        cosine, sine = cos_sin(turns(spots, waves))
        phase_buf[which] = jnp.concatenate([cosine, sine], axis=1)
        return carry

    lax.fori_loop(0, n, phase_step, 0)

    begin = pl.multiple_of(me * waves_each, waves_each)
    own_waves = columns_of(wave_ref[:, pl.ds(begin, waves_each)].astype(jnp.float32))
    factors[...] = jnp.zeros_like(factors)
    gathered[...] = jnp.zeros_like(gathered)
    own_feat.wait()
    own_pos.wait()
    norm_scale = 1.0 / math.sqrt(NBR * BLOCK)

    def shard_step(step, carry):
        @pl.when(step < n)
        def _():
            feat_copy(step).wait_recv()
            forward_copy(step).start()

        now = step - 1

        @pl.when(now > 0)
        def _():
            pos_copy(now).wait_recv()
            forward_copy(now).wait_recv()

        origin = source(now)
        feats = feat_buf[origin].reshape(rows, channels)
        near = rows_of(pos_buf[origin].astype(jnp.float32))
        latent = jnp.dot(feats, fused_w[...], preferred_element_type=jnp.float32)
        cosine, sine = cos_sin(turns(own_waves, near))
        phases = jnp.concatenate([cosine, sine], axis=0)
        factors[...] += jnp.dot(
            phases, latent.astype(jnp.bfloat16), preferred_element_type=jnp.float32
        )
        lane_block = lax.broadcasted_iota(jnp.int32, (1, rows), 1) // BLOCK
        for block in range(blocks_here):
            keep = jnp.zeros((1, rows), jnp.float32)
            for near_block in range(blocks_here):
                number = origin * blocks_here + near_block
                listed = jnp.float32(0.0)
                for slot in range(NBR):
                    listed += jnp.where(nbr_ref[block, slot] == number, norm_scale, 0.0)
                keep = keep + jnp.where(lane_block == near_block, listed, 0.0)
            low = block * BLOCK
            dist_sq = None
            for axis in range(3):
                gap = jnp.abs(spots[axis][low : low + BLOCK] - near[axis]) * (1.0 / 65536.0)
                gap = jnp.minimum(gap, 1.0 - gap)
                dist_sq = gap * gap if dist_sq is None else dist_sq + gap * gap
            distance = jnp.sqrt(dist_sq)
            smooth = jnp.maximum(1.0 - dist_sq * (1.0 / (cutoff * cutoff)), 0.0)
            smooth = smooth * smooth * keep
            for kernel in range(local_kernels):
                center = (group * local_kernels + kernel).astype(jnp.float32) * (
                    cutoff / (RADIAL - 1)
                )
                shaped = (distance - center) / width_ref[kernel]
                weights = (jnp.exp(-(shaped * shaped)) * smooth).astype(jnp.bfloat16)
                gathered[kernel, low : low + BLOCK, :] += jnp.dot(
                    weights, feats, preferred_element_type=jnp.float32
                )
        return carry

    lax.fori_loop(1, n + 1, shard_step, 0)

    lengths = turns(own_waves, own_waves)
    gain = jnp.exp(-lengths * rate_ref[...]) * (1.0 / math.sqrt(rows * n))
    filt_buf[me] = (factors[...] * jnp.concatenate([gain, gain], axis=0)).astype(jnp.bfloat16)
    for step in range(1, n):
        filt_copy(step).start()

    short = jnp.zeros(message.shape, jnp.float32)
    for kernel in range(local_kernels):
        short += jnp.dot(
            gathered[kernel].astype(jnp.bfloat16),
            short_ref[kernel],
            preferred_element_type=jnp.float32,
        )
    message[...] = short
    summed[...] = jnp.dot(phase_buf[me], filt_buf[me], preferred_element_type=jnp.float32)

    def long_step(step, carry):
        filt_copy(step).wait_recv()
        origin = source(step)
        summed[...] += jnp.dot(
            phase_buf[origin], filt_buf[origin], preferred_element_type=jnp.float32
        )
        return carry

    lax.fori_loop(1, n, long_step, 0)

    reduced = (summed[...] * (1.0 / math.sqrt(K))).astype(jnp.bfloat16)
    width = out_ref.shape[1]
    for target in range(groups):
        low = target * width
        part = message[:, low : low + width] + jnp.dot(
            reduced, outw_ref[:, low : low + width], preferred_element_type=jnp.float32
        )
        send_buf[target] = part.astype(jnp.bfloat16)
    for step in range(1, groups):
        msg_copy(step).start()
    total = send_buf[group].astype(jnp.float32)
    for step in range(1, groups):
        msg_copy(step).wait_recv()
        total += recv_buf[step].astype(jnp.float32)
    out_ref[...] = total.astype(out_ref.dtype)
    for step in range(1, n):
        feat_copy(step).wait_send()
        pos_copy(step).wait_send()
        forward_copy(step).wait_send()
        filt_copy(step).wait_send()
    for step in range(1, groups):
        msg_copy(step).wait_send()


def fused(
    features,
    positions,
    neighbours,
    wavevectors,
    radial_width,
    short_weight,
    latent_weight,
    mix_weight,
    filter_rate,
    out_weight,
):
    n = lax.axis_size("atoms")
    groups = lax.axis_size("waves")
    rows, channels = features.shape
    latents = latent_weight.shape[1]
    waves_each = wavevectors.shape[1] // n
    local_kernels = radial_width.shape[0]
    vmem = pl.BlockSpec(memory_space=pltpu.VMEM)
    smem = pl.BlockSpec(memory_space=pltpu.SMEM)
    dma = pltpu.SemaphoreType.DMA
    return pl.pallas_call(
        functools.partial(fused_kernel, n, groups),
        out_shape=jax.ShapeDtypeStruct((rows, channels // groups), jnp.bfloat16),
        in_specs=[vmem, vmem, smem, vmem, smem, vmem, vmem, vmem, vmem, vmem],
        out_specs=vmem,
        scratch_shapes=[
            pltpu.VMEM((n, 2, rows // 2, channels), jnp.bfloat16),
            pltpu.VMEM((n, 3, rows), jnp.int32),
            pltpu.VMEM((channels, latents), jnp.bfloat16),
            pltpu.VMEM((2 * waves_each, latents), jnp.float32),
            pltpu.VMEM((local_kernels, rows, channels), jnp.float32),
            pltpu.VMEM((n, rows, 2 * waves_each), jnp.bfloat16),
            pltpu.VMEM((n, 2 * waves_each, latents), jnp.bfloat16),
            pltpu.VMEM((rows, channels), jnp.float32),
            pltpu.VMEM((rows, latents), jnp.float32),
            pltpu.VMEM((groups, rows, channels // groups), jnp.bfloat16),
            pltpu.VMEM((groups, rows, channels // groups), jnp.bfloat16),
            dma((2,)),
            dma((n,)),
            dma((n,)),
            dma((n,)),
            dma((n,)),
            dma((n,)),
            dma((n,)),
            dma((n,)),
            dma((n,)),
            dma((groups,)),
            dma((groups,)),
        ],
        compiler_params=pltpu.CompilerParams(
            collective_id=0, has_side_effects=True, vmem_limit_bytes=48 * 1024 * 1024
        ),
    )(
        features.reshape(2, rows // 2, channels),
        positions,
        neighbours,
        wavevectors,
        radial_width,
        short_weight,
        latent_weight,
        mix_weight,
        filter_rate.reshape(1, latents),
        out_weight,
    )


def layer(*arrays):
    features, wavevectors = arrays[0], arrays[3]
    n = lax.axis_size("atoms")
    groups = lax.axis_size("waves")
    rows = features.shape[0]
    reach_hops = -(-REACH // (rows // BLOCK))
    covers_all = 2 * reach_hops + 1 >= n
    if covers_all and groups % 2 == 0 and rows % (2 * BLOCK) == 0:
        if wavevectors.shape[1] % (128 * n) == 0:
            return fused(*arrays)
    return local(*arrays)


def solution(mesh):
    placed = (
        P("atoms", None),
        P(None, "atoms"),
        P("atoms", None),
        P(None, "waves"),
        P("waves"),
        P("waves", None, None),
        P(),
        P(),
        P(),
        P(),
    )
    return jax.shard_map(
        layer, mesh=mesh, in_specs=placed, out_specs=P("atoms", "waves"), check_vma=False
    )
```

```python
import functools
import math

import jax
import jax.numpy as jnp
from jax import lax
from jax.experimental import pallas as pl
from jax.experimental.pallas import tpu as pltpu
from jax.sharding import PartitionSpec as P

K = 4096
RADIAL = 8
BLOCK = 128
NBR = 12
REACH = 7


cutoff = 0.5


def shifted(value, axis, steps):
    count = lax.axis_size(axis)
    pairs = [(source, (source + steps) % count) for source in range(count)]
    return lax.ppermute(value, axis, pairs)


def kernels(own_pos, near_pos, centers, radial_width):
    offsets = own_pos[:, None, :, None] - near_pos[:, :, None, :]
    offsets = jnp.mod(offsets, 65536)
    offsets = jnp.where(offsets >= 32768, offsets - 65536, offsets)
    coords = offsets.astype(jnp.float32) * (1.0 / 65536.0)
    dist_sq = jnp.sum(coords * coords, axis=0)
    distance = jnp.sqrt(dist_sq)
    smooth = jnp.where(
        dist_sq < cutoff * cutoff, jnp.square(1.0 - dist_sq / (cutoff * cutoff)), 0.0
    )
    shaped = (distance[None] - centers[:, None, None, None]) / radial_width[:, None, None, None]
    norm_scale = 1.0 / math.sqrt(NBR * BLOCK)
    return (jnp.exp(-jnp.square(shaped)) * smooth[None] * norm_scale).astype(jnp.bfloat16)


def phases_of(wavevectors, spots):
    phase_turn = (
        wavevectors[0][:, None] * spots[0][None, :]
        + wavevectors[1][:, None] * spots[1][None, :]
        + wavevectors[2][:, None] * spots[2][None, :]
    )
    phase_turn = jnp.mod(phase_turn, 65536)
    angles = phase_turn.astype(jnp.float32) * (2.0 * math.pi / 65536.0)
    return jnp.concatenate([jnp.cos(angles), jnp.sin(angles)], axis=0).astype(jnp.bfloat16)


def filter_gain(wavevectors, filter_rate):
    lengths = jnp.sum(wavevectors * wavevectors, axis=0).astype(jnp.float32)
    return jnp.exp(-lengths[:, None] * filter_rate[None, :])


def local(
    features,
    positions,
    neighbours,
    wavevectors,
    radial_width,
    short_weight,
    latent_weight,
    mix_weight,
    filter_rate,
    out_weight,
):
    row_count = features.shape[0]
    channels = features.shape[1]
    blocks_here = row_count // BLOCK
    atom_devices = lax.axis_size("atoms")
    total_blocks = blocks_here * atom_devices
    reach_hops = -(-REACH // blocks_here)
    window_feat = []
    window_pos = []
    for offset in range(-reach_hops, reach_hops + 1):
        if offset == 0:
            arrived = (features, positions)
        else:
            arrived = shifted((features, positions), "atoms", -offset)
        window_feat.append(arrived[0])
        window_pos.append(arrived[1])
    window_feat = jnp.concatenate(window_feat, axis=0).reshape(-1, BLOCK, channels)
    window_pos = jnp.concatenate(window_pos, axis=1).reshape(3, -1, BLOCK)
    first_block = lax.axis_index("atoms") * blocks_here - reach_hops * blocks_here
    local_near = jnp.mod(neighbours - first_block, total_blocks)
    own_pos = positions.reshape(3, blocks_here, BLOCK)
    local_kernels = radial_width.shape[0]
    kernel_ids = lax.axis_index("waves") * local_kernels + jnp.arange(
        local_kernels, dtype=jnp.int32
    )
    centers = cutoff * kernel_ids.astype(jnp.float32) / (RADIAL - 1)
    flat_weight = short_weight.reshape(local_kernels * channels, channels)

    def short_block(block_index):
        near_blocks = local_near[block_index]
        near_feat = window_feat[near_blocks]
        near_pos = window_pos[:, near_blocks]
        weights = kernels(own_pos[:, block_index], near_pos, centers, radial_width)
        gathered = jnp.einsum(
            "rjia,jac->irc", weights, near_feat, preferred_element_type=jnp.float32
        )
        gathered = gathered.astype(jnp.bfloat16).reshape(BLOCK, local_kernels * channels)
        return jnp.dot(gathered, flat_weight, preferred_element_type=jnp.float32)

    short_range = lax.map(short_block, jnp.arange(blocks_here, dtype=jnp.int32)).reshape(
        row_count, channels
    )
    latent = jnp.dot(features, latent_weight, preferred_element_type=jnp.float32).astype(
        jnp.bfloat16
    )
    phases = phases_of(wavevectors, positions)
    partial_factors = jnp.dot(phases, latent, preferred_element_type=jnp.float32)
    gain = filter_gain(wavevectors, filter_rate)
    gain = jnp.concatenate([gain, gain], axis=0)
    norm_scale = 1.0 / math.sqrt(row_count * atom_devices)
    factors = lax.psum(partial_factors, "atoms")
    mixed = jnp.dot(factors, mix_weight, precision=lax.Precision.HIGHEST)
    filtered = (gain * mixed * norm_scale).astype(jnp.bfloat16)
    summed = lax.dot_general(
        phases, filtered, (((0,), (0,)), ((), ())), preferred_element_type=jnp.float32
    )
    summed = (summed * (1.0 / math.sqrt(K))).astype(jnp.bfloat16)
    long_range = jnp.dot(summed, out_weight, preferred_element_type=jnp.float32)
    combined = lax.psum_scatter(
        (short_range + long_range).astype(jnp.bfloat16), "waves", scatter_dimension=1, tiled=True
    )
    return combined


MESH = pl.DeviceIdType.MESH
SINE = (6.28318516, -41.34165503, 81.60100405, -76.5497817, 39.53670129)


def sine_of_turn(quarter):
    square = quarter * quarter
    total = SINE[-1] * square + SINE[-2]
    for factor in SINE[-3::-1]:
        total = total * square + factor
    return total * quarter


def cos_sin(turn):
    turn = turn * (1.0 / 65536.0)
    turn = turn - jnp.floor(turn + 0.5)
    shifted_turn = turn - 0.25
    shifted_turn = jnp.where(shifted_turn < -0.5, shifted_turn + 1.0, shifted_turn)
    return (
        sine_of_turn(0.25 - jnp.abs(turn)).astype(jnp.bfloat16),
        sine_of_turn(0.25 - jnp.abs(shifted_turn)).astype(jnp.bfloat16),
    )


def columns_of(rows):
    padded = jnp.concatenate([rows, jnp.zeros((5, rows.shape[1]), jnp.float32)], axis=0)
    turned = padded.T
    return [turned[:, axis : axis + 1] for axis in range(3)]


def rows_of(rows):
    return [rows[axis : axis + 1, :] for axis in range(3)]


def turns(first, second):
    return first[0] * second[0] + first[1] * second[1] + first[2] * second[2]


def fused_kernel(
    n,
    groups,
    feat_ref,
    pos_ref,
    nbr_ref,
    wave_in,
    width_ref,
    short_in,
    latw_in,
    mix_in,
    rate_in,
    outw_in,
    out_ref,
    wave_ref,
    short_ref,
    latw_ref,
    mix_ref,
    rate_ref,
    outw_ref,
    feat_buf,
    pos_buf,
    fused_w,
    factors,
    gathered,
    phase_buf,
    filt_buf,
    message,
    summed,
    send_buf,
    recv_buf,
    own_sem,
    feat_up,
    feat_down,
    feat_line,
    feat_side_send,
    feat_side,
    pos_send,
    pos_recv,
    fwd_send,
    fwd_recv,
    filt_up,
    filt_down,
    filt_line,
    filt_side_send,
    filt_side,
    msg_send,
    msg_recv,
):
    feat_sends = (feat_up, feat_down, feat_line, feat_side_send, feat_side)
    filt_sends = (filt_up, filt_down, filt_line, filt_side_send, filt_side)
    me = lax.axis_index("atoms")
    group = lax.axis_index("waves")
    core = lax.rem(group, 2)
    partner = group + 1 - 2 * core
    half, channels = feat_ref.shape[1], feat_ref.shape[2]
    rows = 2 * half
    blocks_here = rows // BLOCK
    local_kernels = short_ref.shape[0]
    waves_each = wave_ref.shape[1] // n

    lines = n // 2
    line, side = me // 2, lax.rem(me, 2)

    def peer(step):
        return lax.rem(me + step, n)

    def source(step):
        return lax.rem(me + n - step, n)

    def ranked(rank):
        closest = jnp.minimum(line, lines - 1 - line)
        away = (rank + 1) // 2
        near_line = jnp.where(lax.rem(rank, 2) == 1, line - away, line + away)
        far_line = jnp.where(line < lines - 1 - line, rank, lines - 1 - rank)
        return jnp.where(rank <= 2 * closest, near_line, far_line)

    def line_copy(sends, piece, shard_line, direction):
        up_send, down_send, line_recv, _, _ = sends
        return pltpu.make_async_remote_copy(
            src_ref=piece[0],
            dst_ref=piece[1],
            send_sem=(up_send if direction > 0 else down_send).at[shard_line],
            recv_sem=line_recv.at[shard_line],
            device_id={"atoms": me + 2 * direction},
            device_id_type=MESH,
        )

    def side_copy(sends, piece, shard_line):
        return pltpu.make_async_remote_copy(
            src_ref=piece[0],
            dst_ref=piece[1],
            send_sem=sends[3].at[shard_line],
            recv_sem=sends[4].at[shard_line],
            device_id={"atoms": me + 1 - 2 * side},
            device_id_type=MESH,
        )

    def feat_piece(shard_line, shard_side):
        place = feat_buf.at[2 * shard_line + shard_side, core]
        return place, place

    def filt_piece(shard_line, shard_side):
        place = filt_buf.at[2 * shard_line + shard_side]
        return place, place

    def send_own(sends, piece):
        @pl.when(line < lines - 1)
        def _():
            line_copy(sends, piece, line, 1).start()

        @pl.when(line > 0)
        def _():
            line_copy(sends, piece, line, -1).start()

        side_copy(sends, piece, line).start()

    def pass_on(sends, piece_of, shard_line):
        piece = piece_of(shard_line, side)
        line_copy(sends, piece, shard_line, 1).wait_recv()

        @pl.when((shard_line < line) & (line < lines - 1))
        def _():
            line_copy(sends, piece, shard_line, 1).start()

        @pl.when((shard_line > line) & (line > 0))
        def _():
            line_copy(sends, piece, shard_line, -1).start()

        side_copy(sends, piece, shard_line).start()

    def finish(sends, piece_of):
        def one(shard_line, carry):
            piece = piece_of(shard_line, side)

            @pl.when((shard_line <= line) & (line < lines - 1))
            def _():
                line_copy(sends, piece, shard_line, 1).wait_send()

            @pl.when((shard_line >= line) & (line > 0))
            def _():
                line_copy(sends, piece, shard_line, -1).wait_send()

            side_copy(sends, piece, shard_line).wait_send()
            return carry

        lax.fori_loop(0, lines, one, 0)

    def pos_copy(step):
        return pltpu.make_async_remote_copy(
            src_ref=pos_ref,
            dst_ref=pos_buf.at[me],
            send_sem=pos_send.at[step],
            recv_sem=pos_recv.at[step],
            device_id={"atoms": peer(step)},
            device_id_type=MESH,
        )

    def forward_copy(origin):
        return pltpu.make_async_remote_copy(
            src_ref=feat_buf.at[origin, core],
            dst_ref=feat_buf.at[origin, core],
            send_sem=fwd_send.at[origin],
            recv_sem=fwd_recv.at[origin],
            device_id={"waves": partner},
            device_id_type=MESH,
        )

    def msg_copy(step):
        target = lax.rem(group + step, groups)
        return pltpu.make_async_remote_copy(
            src_ref=send_buf.at[target],
            dst_ref=recv_buf.at[step],
            send_sem=msg_send.at[step],
            recv_sem=msg_recv.at[step],
            device_id={"waves": target},
            device_id_type=MESH,
        )

    own_feat = pltpu.make_async_copy(feat_ref, feat_buf.at[me], own_sem.at[0])
    own_pos = pltpu.make_async_copy(pos_ref, pos_buf.at[me], own_sem.at[1])
    loads = [
        pltpu.make_async_copy(held, kept, own_sem.at[2 + which])
        for which, (held, kept) in enumerate(
            (
                (wave_in, wave_ref),
                (mix_in, mix_ref),
                (latw_in, latw_ref),
                (rate_in, rate_ref),
                (short_in, short_ref),
                (outw_in, outw_ref),
            )
        )
    ]
    own_pos.start()
    for load in loads[:4]:
        load.start()
    own_feat.start()
    for load in loads[4:]:
        load.start()

    barrier = pltpu.get_barrier_semaphore()
    for step in range(1, n):
        pl.semaphore_signal(barrier, inc=1, device_id={"atoms": peer(step)}, device_id_type=MESH)
    for step in range(1, groups):
        pl.semaphore_signal(
            barrier,
            inc=1,
            device_id={"waves": lax.rem(group + step, groups)},
            device_id_type=MESH,
        )
    pl.semaphore_wait(barrier, n - 1 + groups - 1)

    send_own(feat_sends, (feat_ref.at[core], feat_buf.at[me, core]))
    for step in range(1, n):
        pos_copy(step).start()

    own_pos.wait()
    for load in loads[:4]:
        load.wait()
    fused_w[...] = jnp.dot(
        latw_ref[...].astype(jnp.float32),
        mix_ref[...],
        precision=lax.Precision.HIGHEST,
        preferred_element_type=jnp.float32,
    ).astype(jnp.bfloat16)
    spots = columns_of(pos_buf[me].astype(jnp.float32))

    def phase_step(which):
        begin = pl.multiple_of(which * waves_each, waves_each)
        waves = rows_of(wave_ref[:, pl.ds(begin, waves_each)].astype(jnp.float32))
        cosine, sine = cos_sin(turns(spots, waves))
        phase_buf[which] = jnp.concatenate([cosine, sine], axis=1)

    begin = pl.multiple_of(me * waves_each, waves_each)
    own_waves = columns_of(wave_ref[:, pl.ds(begin, waves_each)].astype(jnp.float32))
    factors[...] = jnp.zeros_like(factors)
    gathered[...] = jnp.zeros_like(gathered)
    own_feat.wait()
    norm_scale = 1.0 / math.sqrt(NBR * BLOCK)

    def use_shard(origin):
        phase_step(origin)
        feats = feat_buf[origin].reshape(rows, channels)
        near = rows_of(pos_buf[origin].astype(jnp.float32))
        latent = jnp.dot(feats, fused_w[...], preferred_element_type=jnp.float32)
        cosine, sine = cos_sin(turns(own_waves, near))
        phases = jnp.concatenate([cosine, sine], axis=0)
        factors[...] += jnp.dot(
            phases, latent.astype(jnp.bfloat16), preferred_element_type=jnp.float32
        )
        lane_block = lax.broadcasted_iota(jnp.int32, (1, rows), 1) // BLOCK
        for block in range(blocks_here):
            keep = jnp.zeros((1, rows), jnp.float32)
            for near_block in range(blocks_here):
                number = origin * blocks_here + near_block
                listed = jnp.float32(0.0)
                for slot in range(NBR):
                    listed += jnp.where(nbr_ref[block, slot] == number, norm_scale, 0.0)
                keep = keep + jnp.where(lane_block == near_block, listed, 0.0)
            low = block * BLOCK
            dist_sq = None
            for axis in range(3):
                gap = jnp.abs(spots[axis][low : low + BLOCK] - near[axis]) * (1.0 / 65536.0)
                gap = jnp.minimum(gap, 1.0 - gap)
                dist_sq = gap * gap if dist_sq is None else dist_sq + gap * gap
            distance = jnp.sqrt(dist_sq)
            smooth = jnp.maximum(1.0 - dist_sq * (1.0 / (cutoff * cutoff)), 0.0)
            smooth = smooth * smooth * keep
            for kernel in range(local_kernels):
                center = (group * local_kernels + kernel).astype(jnp.float32) * (
                    cutoff / (RADIAL - 1)
                )
                shaped = (distance - center) * (1.0 / width_ref[kernel])
                weights = (jnp.exp(-(shaped * shaped)) * smooth).astype(jnp.bfloat16)
                gathered[kernel, low : low + BLOCK, :] += jnp.dot(
                    weights, feats, preferred_element_type=jnp.float32
                )

    def gather_step(rank, carry):
        @pl.when(rank < lines)
        def _():
            shard_line = ranked(rank)
            pass_on(feat_sends, feat_piece, shard_line)
            forward_copy(2 * shard_line + side).start()

        shard_line = ranked(rank - 1)
        other = 2 * shard_line + 1 - side
        side_copy(feat_sends, feat_piece(shard_line, 1 - side), shard_line).wait_recv()
        forward_copy(other).start()

        def use_step(which, carry):
            origin = 2 * shard_line + jnp.where(which == 0, side, 1 - side)

            @pl.when(origin != me)
            def _():
                pos_copy(lax.rem(me - origin + n, n)).wait_recv()
                forward_copy(origin).wait_recv()

            use_shard(origin)
            return carry

        lax.fori_loop(0, 2, use_step, 0)
        return carry

    lax.fori_loop(1, lines + 1, gather_step, 0)

    lengths = turns(own_waves, own_waves)
    gain = jnp.exp(-lengths * rate_ref[...]) * (1.0 / math.sqrt(rows * n))
    filt_buf[me] = (factors[...] * jnp.concatenate([gain, gain], axis=0)).astype(jnp.bfloat16)
    send_own(filt_sends, filt_piece(line, side))

    for load in loads[4:]:
        load.wait()
    short = jnp.zeros(message.shape, jnp.float32)
    for kernel in range(local_kernels):
        short += jnp.dot(
            gathered[kernel].astype(jnp.bfloat16),
            short_ref[kernel],
            preferred_element_type=jnp.float32,
        )
    message[...] = short
    summed[...] = jnp.dot(phase_buf[me], filt_buf[me], preferred_element_type=jnp.float32)

    def long_step(rank, carry):
        @pl.when(rank < lines)
        def _():
            pass_on(filt_sends, filt_piece, ranked(rank))

        shard_line = ranked(rank - 1)
        side_copy(filt_sends, filt_piece(shard_line, 1 - side), shard_line).wait_recv()
        other = 2 * shard_line + 1 - side
        summed[...] += jnp.dot(
            phase_buf[other], filt_buf[other], preferred_element_type=jnp.float32
        )

        @pl.when(rank < lines)
        def _():
            origin = 2 * ranked(rank) + side
            summed[...] += jnp.dot(
                phase_buf[origin], filt_buf[origin], preferred_element_type=jnp.float32
            )

        return carry

    lax.fori_loop(1, lines + 1, long_step, 0)

    reduced = (summed[...] * (1.0 / math.sqrt(K))).astype(jnp.bfloat16)
    width = out_ref.shape[1]
    for target in range(groups):
        low = target * width
        part = message[:, low : low + width] + jnp.dot(
            reduced, outw_ref[:, low : low + width], preferred_element_type=jnp.float32
        )
        send_buf[target] = part.astype(jnp.bfloat16)
    for step in range(1, groups):
        msg_copy(step).start()
    total = send_buf[group].astype(jnp.float32)
    for step in range(1, groups):
        msg_copy(step).wait_recv()
        total += recv_buf[step].astype(jnp.float32)
    out_ref[...] = total.astype(out_ref.dtype)
    finish(feat_sends, feat_piece)
    finish(filt_sends, filt_piece)

    def finish_step(step, carry):
        pos_copy(step).wait_send()
        forward_copy(peer(step)).wait_send()
        return carry

    lax.fori_loop(1, n, finish_step, 0)
    for step in range(1, groups):
        msg_copy(step).wait_send()


def fused(
    features,
    positions,
    neighbours,
    wavevectors,
    radial_width,
    short_weight,
    latent_weight,
    mix_weight,
    filter_rate,
    out_weight,
):
    n = lax.axis_size("atoms")
    groups = lax.axis_size("waves")
    rows, channels = features.shape
    latents = latent_weight.shape[1]
    waves_each = wavevectors.shape[1] // n
    local_kernels = radial_width.shape[0]
    vmem = pl.BlockSpec(memory_space=pltpu.VMEM)
    held = pl.BlockSpec(memory_space=pl.ANY)
    smem = pl.BlockSpec(memory_space=pltpu.SMEM)
    dma = pltpu.SemaphoreType.DMA
    return pl.pallas_call(
        functools.partial(fused_kernel, n, groups),
        out_shape=jax.ShapeDtypeStruct((rows, channels // groups), jnp.bfloat16),
        in_specs=[held, held, smem, held, smem, held, held, held, held, held],
        out_specs=vmem,
        scratch_shapes=[
            pltpu.VMEM(wavevectors.shape, jnp.int32),
            pltpu.VMEM(short_weight.shape, jnp.bfloat16),
            pltpu.VMEM(latent_weight.shape, jnp.bfloat16),
            pltpu.VMEM(mix_weight.shape, jnp.float32),
            pltpu.VMEM((1, latents), jnp.float32),
            pltpu.VMEM(out_weight.shape, jnp.bfloat16),
            pltpu.VMEM((n, 2, rows // 2, channels), jnp.bfloat16),
            pltpu.VMEM((n, 3, rows), jnp.int32),
            pltpu.VMEM((channels, latents), jnp.bfloat16),
            pltpu.VMEM((2 * waves_each, latents), jnp.float32),
            pltpu.VMEM((local_kernels, rows, channels), jnp.float32),
            pltpu.VMEM((n, rows, 2 * waves_each), jnp.bfloat16),
            pltpu.VMEM((n, 2 * waves_each, latents), jnp.bfloat16),
            pltpu.VMEM((rows, channels), jnp.float32),
            pltpu.VMEM((rows, latents), jnp.float32),
            pltpu.VMEM((groups, rows, channels // groups), jnp.bfloat16),
            pltpu.VMEM((groups, rows, channels // groups), jnp.bfloat16),
            dma((8,)),
            *[dma((n // 2,)) for _ in range(5)],
            *[dma((n,)) for _ in range(4)],
            *[dma((n // 2,)) for _ in range(5)],
            *[dma((groups,)) for _ in range(2)],
        ],
        compiler_params=pltpu.CompilerParams(
            collective_id=0, has_side_effects=True, vmem_limit_bytes=67043328
        ),
    )(
        features.reshape(2, rows // 2, channels),
        positions,
        neighbours,
        wavevectors,
        radial_width,
        short_weight,
        latent_weight,
        mix_weight,
        filter_rate.reshape(1, latents),
        out_weight,
    )


def layer(*arrays):
    features, wavevectors = arrays[0], arrays[3]
    n = lax.axis_size("atoms")
    groups = lax.axis_size("waves")
    rows = features.shape[0]
    reach_hops = -(-REACH // (rows // BLOCK))
    covers_all = 2 * reach_hops + 1 >= n
    if covers_all and groups % 2 == 0 and n % 2 == 0 and rows % (2 * BLOCK) == 0:
        if wavevectors.shape[1] % (128 * n) == 0:
            return fused(*arrays)
    return local(*arrays)


def solution(mesh):
    placed = (
        P("atoms", None),
        P(None, "atoms"),
        P("atoms", None),
        P(None, "waves"),
        P("waves"),
        P("waves", None, None),
        P(),
        P(),
        P(),
        P(),
    )
    return jax.shard_map(
        layer, mesh=mesh, in_specs=placed, out_specs=P("atoms", "waves"), check_vma=False
    )
```

```python
import functools
import math

import jax
import jax.numpy as jnp
from jax import lax
from jax.experimental import pallas as pl
from jax.experimental.pallas import tpu as pltpu
from jax.sharding import PartitionSpec as P

K = 4096
RADIAL = 8
BLOCK = 128
NBR = 12
REACH = 7


cutoff = 0.5


def shifted(value, axis, steps):
    count = lax.axis_size(axis)
    pairs = [(source, (source + steps) % count) for source in range(count)]
    return lax.ppermute(value, axis, pairs)


def kernels(own_pos, near_pos, centers, radial_width):
    offsets = own_pos[:, None, :, None] - near_pos[:, :, None, :]
    offsets = jnp.mod(offsets, 65536)
    offsets = jnp.where(offsets >= 32768, offsets - 65536, offsets)
    coords = offsets.astype(jnp.float32) * (1.0 / 65536.0)
    dist_sq = jnp.sum(coords * coords, axis=0)
    distance = jnp.sqrt(dist_sq)
    smooth = jnp.where(
        dist_sq < cutoff * cutoff, jnp.square(1.0 - dist_sq / (cutoff * cutoff)), 0.0
    )
    shaped = (distance[None] - centers[:, None, None, None]) / radial_width[:, None, None, None]
    norm_scale = 1.0 / math.sqrt(NBR * BLOCK)
    return (jnp.exp(-jnp.square(shaped)) * smooth[None] * norm_scale).astype(jnp.bfloat16)


def phases_of(wavevectors, spots):
    phase_turn = (
        wavevectors[0][:, None] * spots[0][None, :]
        + wavevectors[1][:, None] * spots[1][None, :]
        + wavevectors[2][:, None] * spots[2][None, :]
    )
    phase_turn = jnp.mod(phase_turn, 65536)
    angles = phase_turn.astype(jnp.float32) * (2.0 * math.pi / 65536.0)
    return jnp.concatenate([jnp.cos(angles), jnp.sin(angles)], axis=0).astype(jnp.bfloat16)


def filter_gain(wavevectors, filter_rate):
    lengths = jnp.sum(wavevectors * wavevectors, axis=0).astype(jnp.float32)
    return jnp.exp(-lengths[:, None] * filter_rate[None, :])


def local(
    features,
    positions,
    neighbours,
    wavevectors,
    radial_width,
    short_weight,
    latent_weight,
    mix_weight,
    filter_rate,
    out_weight,
):
    row_count = features.shape[0]
    channels = features.shape[1]
    blocks_here = row_count // BLOCK
    atom_devices = lax.axis_size("atoms")
    total_blocks = blocks_here * atom_devices
    reach_hops = -(-REACH // blocks_here)
    window_feat = []
    window_pos = []
    for offset in range(-reach_hops, reach_hops + 1):
        if offset == 0:
            arrived = (features, positions)
        else:
            arrived = shifted((features, positions), "atoms", -offset)
        window_feat.append(arrived[0])
        window_pos.append(arrived[1])
    window_feat = jnp.concatenate(window_feat, axis=0).reshape(-1, BLOCK, channels)
    window_pos = jnp.concatenate(window_pos, axis=1).reshape(3, -1, BLOCK)
    first_block = lax.axis_index("atoms") * blocks_here - reach_hops * blocks_here
    local_near = jnp.mod(neighbours - first_block, total_blocks)
    own_pos = positions.reshape(3, blocks_here, BLOCK)
    local_kernels = radial_width.shape[0]
    kernel_ids = lax.axis_index("waves") * local_kernels + jnp.arange(
        local_kernels, dtype=jnp.int32
    )
    centers = cutoff * kernel_ids.astype(jnp.float32) / (RADIAL - 1)
    flat_weight = short_weight.reshape(local_kernels * channels, channels)

    def short_block(block_index):
        near_blocks = local_near[block_index]
        near_feat = window_feat[near_blocks]
        near_pos = window_pos[:, near_blocks]
        weights = kernels(own_pos[:, block_index], near_pos, centers, radial_width)
        gathered = jnp.einsum(
            "rjia,jac->irc", weights, near_feat, preferred_element_type=jnp.float32
        )
        gathered = gathered.astype(jnp.bfloat16).reshape(BLOCK, local_kernels * channels)
        return jnp.dot(gathered, flat_weight, preferred_element_type=jnp.float32)

    short_range = lax.map(short_block, jnp.arange(blocks_here, dtype=jnp.int32)).reshape(
        row_count, channels
    )
    latent = jnp.dot(features, latent_weight, preferred_element_type=jnp.float32).astype(
        jnp.bfloat16
    )
    phases = phases_of(wavevectors, positions)
    partial_factors = jnp.dot(phases, latent, preferred_element_type=jnp.float32)
    gain = filter_gain(wavevectors, filter_rate)
    gain = jnp.concatenate([gain, gain], axis=0)
    norm_scale = 1.0 / math.sqrt(row_count * atom_devices)
    factors = lax.psum(partial_factors, "atoms")
    mixed = jnp.dot(factors, mix_weight, precision=lax.Precision.HIGHEST)
    filtered = (gain * mixed * norm_scale).astype(jnp.bfloat16)
    summed = lax.dot_general(
        phases, filtered, (((0,), (0,)), ((), ())), preferred_element_type=jnp.float32
    )
    summed = (summed * (1.0 / math.sqrt(K))).astype(jnp.bfloat16)
    long_range = jnp.dot(summed, out_weight, preferred_element_type=jnp.float32)
    combined = lax.psum_scatter(
        (short_range + long_range).astype(jnp.bfloat16), "waves", scatter_dimension=1, tiled=True
    )
    return combined


MESH = pl.DeviceIdType.MESH
SINE = (6.28318516, -41.34165503, 81.60100405, -76.5497817, 39.53670129)


def sine_of_turn(quarter):
    square = quarter * quarter
    total = SINE[-1] * square + SINE[-2]
    for factor in SINE[-3::-1]:
        total = total * square + factor
    return total * quarter


def cos_sin(turn):
    turn = turn * (1.0 / 65536.0)
    turn = turn - jnp.floor(turn + 0.5)
    shifted_turn = turn - 0.25
    shifted_turn = jnp.where(shifted_turn < -0.5, shifted_turn + 1.0, shifted_turn)
    return (
        sine_of_turn(0.25 - jnp.abs(turn)).astype(jnp.bfloat16),
        sine_of_turn(0.25 - jnp.abs(shifted_turn)).astype(jnp.bfloat16),
    )


def columns_of(rows):
    padded = jnp.concatenate([rows, jnp.zeros((5, rows.shape[1]), jnp.float32)], axis=0)
    turned = padded.T
    return [turned[:, axis : axis + 1] for axis in range(3)]


def rows_of(rows):
    return [rows[axis : axis + 1, :] for axis in range(3)]


def turns(first, second):
    return first[0] * second[0] + first[1] * second[1] + first[2] * second[2]


def fused_kernel(
    n,
    groups,
    feat_ref,
    pos_ref,
    nbr_ref,
    wave_in,
    width_ref,
    short_in,
    latw_in,
    mix_in,
    rate_in,
    outw_in,
    out_ref,
    wave_ref,
    short_ref,
    latw_ref,
    mix_ref,
    rate_ref,
    outw_ref,
    feat_buf,
    pos_buf,
    fused_w,
    factors,
    gathered,
    phase_buf,
    wave_cols,
    filt_cols,
    filt_buf,
    sum_send_buf,
    sum_buf,
    message,
    summed,
    send_buf,
    recv_buf,
    own_sem,
    feat_up,
    feat_down,
    feat_line,
    feat_side_send,
    feat_side,
    pos_send,
    pos_recv,
    fwd_send,
    fwd_recv,
    sum_send,
    sum_recv,
    msg_send,
    msg_recv,
):
    feat_sends = (feat_up, feat_down, feat_line, feat_side_send, feat_side)
    me = lax.axis_index("atoms")
    group = lax.axis_index("waves")
    core = lax.rem(group, 2)
    partner = group + 1 - 2 * core
    half, channels = feat_ref.shape[1], feat_ref.shape[2]
    rows = 2 * half
    blocks_here = rows // BLOCK
    local_kernels = short_ref.shape[0]
    waves_each = wave_ref.shape[1] // 2
    part = mix_ref.shape[1] // (n // 2)
    per_tile = 128 // part

    lines = n // 2
    line, side = me // 2, lax.rem(me, 2)

    def peer(step):
        return lax.rem(me + step, n)

    def source(step):
        return lax.rem(me + n - step, n)

    def ranked(rank):
        closest = jnp.minimum(line, lines - 1 - line)
        away = (rank + 1) // 2
        near_line = jnp.where(lax.rem(rank, 2) == 1, line - away, line + away)
        far_line = jnp.where(line < lines - 1 - line, rank, lines - 1 - rank)
        return jnp.where(rank <= 2 * closest, near_line, far_line)

    def line_copy(sends, piece, shard_line, direction):
        up_send, down_send, line_recv, _, _ = sends
        return pltpu.make_async_remote_copy(
            src_ref=piece[0],
            dst_ref=piece[1],
            send_sem=(up_send if direction > 0 else down_send).at[shard_line],
            recv_sem=line_recv.at[shard_line],
            device_id={"atoms": me + 2 * direction},
            device_id_type=MESH,
        )

    def side_copy(sends, piece, shard_line):
        return pltpu.make_async_remote_copy(
            src_ref=piece[0],
            dst_ref=piece[1],
            send_sem=sends[3].at[shard_line],
            recv_sem=sends[4].at[shard_line],
            device_id={"atoms": me + 1 - 2 * side},
            device_id_type=MESH,
        )

    def feat_piece(shard_line, shard_side):
        place = feat_buf.at[2 * shard_line + shard_side, core]
        return place, place

    def send_own(sends, piece):
        @pl.when(line < lines - 1)
        def _():
            line_copy(sends, piece, line, 1).start()

        @pl.when(line > 0)
        def _():
            line_copy(sends, piece, line, -1).start()

        side_copy(sends, piece, line).start()

    def pass_on(sends, piece_of, shard_line):
        piece = piece_of(shard_line, side)
        line_copy(sends, piece, shard_line, 1).wait_recv()

        @pl.when((shard_line < line) & (line < lines - 1))
        def _():
            line_copy(sends, piece, shard_line, 1).start()

        @pl.when((shard_line > line) & (line > 0))
        def _():
            line_copy(sends, piece, shard_line, -1).start()

        side_copy(sends, piece, shard_line).start()

    def finish(sends, piece_of):
        def one(shard_line, carry):
            piece = piece_of(shard_line, side)

            @pl.when((shard_line <= line) & (line < lines - 1))
            def _():
                line_copy(sends, piece, shard_line, 1).wait_send()

            @pl.when((shard_line >= line) & (line > 0))
            def _():
                line_copy(sends, piece, shard_line, -1).wait_send()

            side_copy(sends, piece, shard_line).wait_send()
            return carry

        lax.fori_loop(0, lines, one, 0)

    def pos_copy(step):
        return pltpu.make_async_remote_copy(
            src_ref=pos_ref,
            dst_ref=pos_buf.at[me],
            send_sem=pos_send.at[step],
            recv_sem=pos_recv.at[step],
            device_id={"atoms": peer(step)},
            device_id_type=MESH,
        )

    def forward_copy(origin):
        return pltpu.make_async_remote_copy(
            src_ref=feat_buf.at[origin, core],
            dst_ref=feat_buf.at[origin, core],
            send_sem=fwd_send.at[origin],
            recv_sem=fwd_recv.at[origin],
            device_id={"waves": partner},
            device_id_type=MESH,
        )

    def sum_copy(step):
        return pltpu.make_async_remote_copy(
            src_ref=sum_send_buf.at[peer(step)],
            dst_ref=sum_buf.at[me],
            send_sem=sum_send.at[step],
            recv_sem=sum_recv.at[step],
            device_id={"atoms": peer(step)},
            device_id_type=MESH,
        )

    def msg_copy(step):
        target = lax.rem(group + step, groups)
        return pltpu.make_async_remote_copy(
            src_ref=send_buf.at[target],
            dst_ref=recv_buf.at[step],
            send_sem=msg_send.at[step],
            recv_sem=msg_recv.at[step],
            device_id={"waves": target},
            device_id_type=MESH,
        )

    own_feat = pltpu.make_async_copy(feat_ref, feat_buf.at[me], own_sem.at[0])
    own_pos = pltpu.make_async_copy(pos_ref, pos_buf.at[me], own_sem.at[1])
    loads = [
        pltpu.make_async_copy(held, kept, own_sem.at[2 + which])
        for which, (held, kept) in enumerate(
            (
                (wave_in, wave_ref),
                (mix_in, mix_ref),
                (latw_in, latw_ref),
                (rate_in, rate_ref),
                (short_in, short_ref),
                (outw_in, outw_ref),
            )
        )
    ]
    own_pos.start()
    for load in loads[:4]:
        load.start()
    own_feat.start()
    for load in loads[4:]:
        load.start()

    barrier = pltpu.get_barrier_semaphore()
    for step in range(1, n):
        pl.semaphore_signal(barrier, inc=1, device_id={"atoms": peer(step)}, device_id_type=MESH)
    for step in range(1, groups):
        pl.semaphore_signal(
            barrier,
            inc=1,
            device_id={"waves": lax.rem(group + step, groups)},
            device_id_type=MESH,
        )
    pl.semaphore_wait(barrier, n - 1 + groups - 1)

    send_own(feat_sends, (feat_ref.at[core], feat_buf.at[me, core]))
    for step in range(1, n):
        pos_copy(step).start()

    own_pos.wait()
    for load in loads[:4]:
        load.wait()
    tile = pl.ds(pl.multiple_of((line // per_tile) * 128, 128), 128)
    fused_w[...] = jnp.dot(
        latw_ref[...].astype(jnp.float32),
        mix_ref[:, tile],
        precision=lax.Precision.HIGHEST,
        preferred_element_type=jnp.float32,
    ).astype(jnp.bfloat16)
    spots = columns_of(pos_buf[me].astype(jnp.float32))

    begin = pl.multiple_of(side * waves_each, waves_each)
    own_waves = columns_of(wave_ref[:, pl.ds(begin, waves_each)].astype(jnp.float32))
    for axis in range(3):
        wave_cols[axis] = jnp.broadcast_to(own_waves[axis], (waves_each, 128))
    chunk = 64

    def phase_rows(origin, near):
        def some(which, carry):
            low = pl.multiple_of(which * chunk, chunk)
            waves = [wave_cols[axis, pl.ds(low, chunk), :] for axis in range(3)]
            for start in range(0, rows, 128):
                spot = [row[:, start : start + 128] for row in near]
                cosine, sine = cos_sin(turns(waves, spot))
                phase_buf[origin, pl.ds(low, chunk), start : start + 128] = cosine
                high = pl.multiple_of(waves_each + low, chunk)
                phase_buf[origin, pl.ds(high, chunk), start : start + 128] = sine
            return carry

        lax.fori_loop(0, waves_each // chunk, some, 0)

    factors[...] = jnp.zeros_like(factors)
    gathered[...] = jnp.zeros_like(gathered)
    own_feat.wait()
    norm_scale = 1.0 / math.sqrt(NBR * BLOCK)

    def use_shard(origin):
        feats = feat_buf[origin].reshape(rows, channels)
        near = rows_of(pos_buf[origin].astype(jnp.float32))
        latent = jnp.dot(feats, fused_w[...], preferred_element_type=jnp.float32)
        phase_rows(origin, near)
        factors[...] += jnp.dot(
            phase_buf[origin], latent.astype(jnp.bfloat16), preferred_element_type=jnp.float32
        )
        lane_block = lax.broadcasted_iota(jnp.int32, (1, rows), 1) // BLOCK
        for block in range(blocks_here):
            keep = jnp.zeros((1, rows), jnp.float32)
            for near_block in range(blocks_here):
                number = origin * blocks_here + near_block
                listed = jnp.float32(0.0)
                for slot in range(NBR):
                    listed += jnp.where(nbr_ref[block, slot] == number, norm_scale, 0.0)
                keep = keep + jnp.where(lane_block == near_block, listed, 0.0)
            low = block * BLOCK
            dist_sq = None
            for axis in range(3):
                gap = jnp.abs(spots[axis][low : low + BLOCK] - near[axis]) * (1.0 / 65536.0)
                gap = jnp.minimum(gap, 1.0 - gap)
                dist_sq = gap * gap if dist_sq is None else dist_sq + gap * gap
            distance = jnp.sqrt(dist_sq)
            smooth = jnp.maximum(1.0 - dist_sq * (1.0 / (cutoff * cutoff)), 0.0)
            smooth = smooth * smooth * keep
            for kernel in range(local_kernels):
                center = (group * local_kernels + kernel).astype(jnp.float32) * (
                    cutoff / (RADIAL - 1)
                )
                shaped = (distance - center) * (1.0 / width_ref[kernel])
                weights = (jnp.exp(-(shaped * shaped)) * smooth).astype(jnp.bfloat16)
                gathered[kernel, low : low + BLOCK, :] += jnp.dot(
                    weights, feats, preferred_element_type=jnp.float32
                )

    use_shard(me)

    def gather_step(rank, carry):
        @pl.when(rank < lines)
        def _():
            shard_line = ranked(rank)
            pass_on(feat_sends, feat_piece, shard_line)
            forward_copy(2 * shard_line + side).start()

        shard_line = ranked(rank - 1)
        other = 2 * shard_line + 1 - side
        side_copy(feat_sends, feat_piece(shard_line, 1 - side), shard_line).wait_recv()
        forward_copy(other).start()

        def use_step(which, carry):
            origin = jnp.where(which == 0, 2 * ranked(rank) + side, other)
            pos_copy(lax.rem(me - origin + n, n)).wait_recv()
            forward_copy(origin).wait_recv()
            use_shard(origin)
            return carry

        lax.fori_loop(rank // lines, 2, use_step, 0)
        return carry

    lax.fori_loop(1, lines + 1, gather_step, 0)

    lengths = turns(own_waves, own_waves)
    gain = jnp.exp(-lengths * rate_ref[:, tile]) * (1.0 / math.sqrt(rows * n))
    filt_cols[...] = (factors[...] * jnp.concatenate([gain, gain], axis=0)).T
    turned = filt_cols[pl.ds(pl.multiple_of(lax.rem(line, per_tile) * part, part), part), :]
    filt_buf[...] = turned.astype(jnp.bfloat16)

    def sum_of(owner):
        sums = jnp.dot(filt_buf[...], phase_buf[owner], preferred_element_type=jnp.float32)
        return (sums * (1.0 / math.sqrt(K))).astype(jnp.bfloat16)

    def sum_step(step, carry):
        sum_send_buf[peer(step)] = sum_of(peer(step))
        sum_copy(step).start()
        return carry

    lax.fori_loop(1, n, sum_step, 0)
    sum_buf[me] = sum_of(me)
    for load in loads[4:]:
        load.wait()
    short = jnp.zeros(message.shape, jnp.float32)
    for kernel in range(local_kernels):
        short += jnp.dot(
            gathered[kernel].astype(jnp.bfloat16),
            short_ref[kernel],
            preferred_element_type=jnp.float32,
        )
    message[...] = short
    for step in range(1, n):
        sum_copy(step).wait_recv()
    for whole in range(lines):
        summed[whole * part : (whole + 1) * part, :] = sum_buf[2 * whole].astype(
            jnp.float32
        ) + sum_buf[2 * whole + 1].astype(jnp.float32)
    reduced = summed[...].T.astype(jnp.bfloat16)
    width = out_ref.shape[1]
    for target in range(groups):
        low = target * width
        part = message[:, low : low + width] + jnp.dot(
            reduced, outw_ref[:, low : low + width], preferred_element_type=jnp.float32
        )
        send_buf[target] = part.astype(jnp.bfloat16)
    for step in range(1, groups):
        msg_copy(step).start()
    total = send_buf[group].astype(jnp.float32)
    for step in range(1, groups):
        msg_copy(step).wait_recv()
        total += recv_buf[step].astype(jnp.float32)
    out_ref[...] = total.astype(out_ref.dtype)
    finish(feat_sends, feat_piece)

    def finish_step(step, carry):
        pos_copy(step).wait_send()
        sum_copy(step).wait_send()
        forward_copy(peer(step)).wait_send()
        return carry

    lax.fori_loop(1, n, finish_step, 0)
    for step in range(1, groups):
        msg_copy(step).wait_send()


def fused(
    features,
    positions,
    neighbours,
    wavevectors,
    radial_width,
    short_weight,
    latent_weight,
    mix_weight,
    filter_rate,
    out_weight,
):
    n = lax.axis_size("atoms")
    groups = lax.axis_size("waves")
    rows, channels = features.shape
    latents = latent_weight.shape[1]
    waves_each = wavevectors.shape[1] // 2
    part = latents // (n // 2)
    local_kernels = radial_width.shape[0]
    vmem = pl.BlockSpec(memory_space=pltpu.VMEM)
    held = pl.BlockSpec(memory_space=pl.ANY)
    smem = pl.BlockSpec(memory_space=pltpu.SMEM)
    dma = pltpu.SemaphoreType.DMA
    return pl.pallas_call(
        functools.partial(fused_kernel, n, groups),
        out_shape=jax.ShapeDtypeStruct((rows, channels // groups), jnp.bfloat16),
        in_specs=[held, held, smem, held, smem, held, held, held, held, held],
        out_specs=vmem,
        scratch_shapes=[
            pltpu.VMEM(wavevectors.shape, jnp.int32),
            pltpu.VMEM(short_weight.shape, jnp.bfloat16),
            pltpu.VMEM(latent_weight.shape, jnp.bfloat16),
            pltpu.VMEM(mix_weight.shape, jnp.float32),
            pltpu.VMEM((1, latents), jnp.float32),
            pltpu.VMEM(out_weight.shape, jnp.bfloat16),
            pltpu.VMEM((n, 2, rows // 2, channels), jnp.bfloat16),
            pltpu.VMEM((n, 3, rows), jnp.int32),
            pltpu.VMEM((channels, 128), jnp.bfloat16),
            pltpu.VMEM((2 * waves_each, 128), jnp.float32),
            pltpu.VMEM((local_kernels, rows, channels), jnp.float32),
            pltpu.VMEM((n, 2 * waves_each, rows), jnp.bfloat16),
            pltpu.VMEM((3, waves_each, 128), jnp.float32),
            pltpu.VMEM((128, 2 * waves_each), jnp.float32),
            pltpu.VMEM((part, 2 * waves_each), jnp.bfloat16),
            pltpu.VMEM((n, part, rows), jnp.bfloat16),
            pltpu.VMEM((n, part, rows), jnp.bfloat16),
            pltpu.VMEM((rows, channels), jnp.float32),
            pltpu.VMEM((latents, rows), jnp.float32),
            pltpu.VMEM((groups, rows, channels // groups), jnp.bfloat16),
            pltpu.VMEM((groups, rows, channels // groups), jnp.bfloat16),
            dma((8,)),
            *[dma((n // 2,)) for _ in range(5)],
            *[dma((n,)) for _ in range(4)],
            *[dma((n,)) for _ in range(2)],
            *[dma((groups,)) for _ in range(2)],
        ],
        compiler_params=pltpu.CompilerParams(
            collective_id=0, has_side_effects=True, vmem_limit_bytes=67043328
        ),
    )(
        features.reshape(2, rows // 2, channels),
        positions,
        neighbours,
        wavevectors,
        radial_width,
        short_weight,
        latent_weight,
        mix_weight,
        filter_rate.reshape(1, latents),
        out_weight,
    )


def layer(*arrays):
    features, wavevectors = arrays[0], arrays[3]
    n = lax.axis_size("atoms")
    groups = lax.axis_size("waves")
    rows = features.shape[0]
    reach_hops = -(-REACH // (rows // BLOCK))
    covers_all = 2 * reach_hops + 1 >= n
    if covers_all and groups % 2 == 0 and n % 2 == 0 and rows % (2 * BLOCK) == 0:
        lines = n // 2
        latents = arrays[6].shape[1]
        part = latents // lines
        if wavevectors.shape[1] % 256 == 0 and part in (32, 64, 128) and part * lines == latents:
            return fused(*arrays)
    return local(*arrays)


def solution(mesh):
    placed = (
        P("atoms", None),
        P(None, "atoms"),
        P("atoms", None),
        P(None, "waves"),
        P("waves"),
        P("waves", None, None),
        P(),
        P(),
        P(),
        P(),
    )
    return jax.shard_map(
        layer, mesh=mesh, in_specs=placed, out_specs=P("atoms", "waves"), check_vma=False
    )
```

```python
import functools
import math

import jax
import jax.numpy as jnp
from jax import lax
from jax.experimental import pallas as pl
from jax.experimental.pallas import tpu as pltpu
from jax.sharding import PartitionSpec as P

K = 4096
RADIAL = 8
BLOCK = 128
NBR = 12
REACH = 7


cutoff = 0.5


def shifted(value, axis, steps):
    count = lax.axis_size(axis)
    pairs = [(source, (source + steps) % count) for source in range(count)]
    return lax.ppermute(value, axis, pairs)


def kernels(own_pos, near_pos, centers, radial_width):
    offsets = own_pos[:, None, :, None] - near_pos[:, :, None, :]
    offsets = jnp.mod(offsets, 65536)
    offsets = jnp.where(offsets >= 32768, offsets - 65536, offsets)
    coords = offsets.astype(jnp.float32) * (1.0 / 65536.0)
    dist_sq = jnp.sum(coords * coords, axis=0)
    distance = jnp.sqrt(dist_sq)
    smooth = jnp.where(
        dist_sq < cutoff * cutoff, jnp.square(1.0 - dist_sq / (cutoff * cutoff)), 0.0
    )
    shaped = (distance[None] - centers[:, None, None, None]) / radial_width[:, None, None, None]
    norm_scale = 1.0 / math.sqrt(NBR * BLOCK)
    return (jnp.exp(-jnp.square(shaped)) * smooth[None] * norm_scale).astype(jnp.bfloat16)


def phases_of(wavevectors, spots):
    phase_turn = (
        wavevectors[0][:, None] * spots[0][None, :]
        + wavevectors[1][:, None] * spots[1][None, :]
        + wavevectors[2][:, None] * spots[2][None, :]
    )
    phase_turn = jnp.mod(phase_turn, 65536)
    angles = phase_turn.astype(jnp.float32) * (2.0 * math.pi / 65536.0)
    return jnp.concatenate([jnp.cos(angles), jnp.sin(angles)], axis=0).astype(jnp.bfloat16)


def filter_gain(wavevectors, filter_rate):
    lengths = jnp.sum(wavevectors * wavevectors, axis=0).astype(jnp.float32)
    return jnp.exp(-lengths[:, None] * filter_rate[None, :])


def local(
    features,
    positions,
    neighbours,
    wavevectors,
    radial_width,
    short_weight,
    latent_weight,
    mix_weight,
    filter_rate,
    out_weight,
):
    row_count = features.shape[0]
    channels = features.shape[1]
    blocks_here = row_count // BLOCK
    atom_devices = lax.axis_size("atoms")
    total_blocks = blocks_here * atom_devices
    reach_hops = -(-REACH // blocks_here)
    window_feat = []
    window_pos = []
    for offset in range(-reach_hops, reach_hops + 1):
        if offset == 0:
            arrived = (features, positions)
        else:
            arrived = shifted((features, positions), "atoms", -offset)
        window_feat.append(arrived[0])
        window_pos.append(arrived[1])
    window_feat = jnp.concatenate(window_feat, axis=0).reshape(-1, BLOCK, channels)
    window_pos = jnp.concatenate(window_pos, axis=1).reshape(3, -1, BLOCK)
    first_block = lax.axis_index("atoms") * blocks_here - reach_hops * blocks_here
    local_near = jnp.mod(neighbours - first_block, total_blocks)
    own_pos = positions.reshape(3, blocks_here, BLOCK)
    local_kernels = radial_width.shape[0]
    kernel_ids = lax.axis_index("waves") * local_kernels + jnp.arange(
        local_kernels, dtype=jnp.int32
    )
    centers = cutoff * kernel_ids.astype(jnp.float32) / (RADIAL - 1)
    flat_weight = short_weight.reshape(local_kernels * channels, channels)

    def short_block(block_index):
        near_blocks = local_near[block_index]
        near_feat = window_feat[near_blocks]
        near_pos = window_pos[:, near_blocks]
        weights = kernels(own_pos[:, block_index], near_pos, centers, radial_width)
        gathered = jnp.einsum(
            "rjia,jac->irc", weights, near_feat, preferred_element_type=jnp.float32
        )
        gathered = gathered.astype(jnp.bfloat16).reshape(BLOCK, local_kernels * channels)
        return jnp.dot(gathered, flat_weight, preferred_element_type=jnp.float32)

    short_range = lax.map(short_block, jnp.arange(blocks_here, dtype=jnp.int32)).reshape(
        row_count, channels
    )
    latent = jnp.dot(features, latent_weight, preferred_element_type=jnp.float32).astype(
        jnp.bfloat16
    )
    phases = phases_of(wavevectors, positions)
    partial_factors = jnp.dot(phases, latent, preferred_element_type=jnp.float32)
    gain = filter_gain(wavevectors, filter_rate)
    gain = jnp.concatenate([gain, gain], axis=0)
    norm_scale = 1.0 / math.sqrt(row_count * atom_devices)
    factors = lax.psum(partial_factors, "atoms")
    mixed = jnp.dot(factors, mix_weight, precision=lax.Precision.HIGHEST)
    filtered = (gain * mixed * norm_scale).astype(jnp.bfloat16)
    summed = lax.dot_general(
        phases, filtered, (((0,), (0,)), ((), ())), preferred_element_type=jnp.float32
    )
    summed = (summed * (1.0 / math.sqrt(K))).astype(jnp.bfloat16)
    long_range = jnp.dot(summed, out_weight, preferred_element_type=jnp.float32)
    combined = lax.psum_scatter(
        (short_range + long_range).astype(jnp.bfloat16), "waves", scatter_dimension=1, tiled=True
    )
    return combined


MESH = pl.DeviceIdType.MESH
PIECES = 4
SINE = (6.28318516, -41.34165503, 81.60100405, -76.5497817, 39.53670129)


def sine_of_turn(quarter):
    square = quarter * quarter
    total = SINE[-1] * square + SINE[-2]
    for factor in SINE[-3::-1]:
        total = total * square + factor
    return total * quarter


def cos_sin(turn):
    turn = turn * (1.0 / 65536.0)
    turn = turn - jnp.floor(turn + 0.5)
    shifted_turn = turn - 0.25
    shifted_turn = jnp.where(shifted_turn < -0.5, shifted_turn + 1.0, shifted_turn)
    return (
        sine_of_turn(0.25 - jnp.abs(turn)).astype(jnp.bfloat16),
        sine_of_turn(0.25 - jnp.abs(shifted_turn)).astype(jnp.bfloat16),
    )


def columns_of(rows):
    padded = jnp.concatenate([rows, jnp.zeros((5, rows.shape[1]), jnp.float32)], axis=0)
    turned = padded.T
    return [turned[:, axis : axis + 1] for axis in range(3)]


def rows_of(rows):
    return [rows[axis : axis + 1, :] for axis in range(3)]


def turns(first, second):
    return first[0] * second[0] + first[1] * second[1] + first[2] * second[2]


def fused_kernel(
    n,
    groups,
    feat_ref,
    pos_ref,
    nbr_ref,
    wave_in,
    width_ref,
    short_in,
    latw_in,
    mix_in,
    rate_in,
    outw_in,
    out_ref,
    wave_ref,
    short_ref,
    latw_ref,
    mix_ref,
    rate_ref,
    outw_ref,
    feat_buf,
    pos_buf,
    fused_w,
    factors,
    gathered,
    phase_buf,
    wave_cols,
    filt_cols,
    filt_buf,
    sum_send_buf,
    sum_buf,
    message,
    summed,
    send_buf,
    recv_buf,
    own_sem,
    feat_up,
    feat_down,
    feat_line,
    feat_side_send,
    feat_side,
    pos_send,
    pos_recv,
    fwd_send,
    fwd_recv,
    sum_send,
    sum_recv,
    msg_send,
    msg_recv,
):
    feat_sends = (feat_up, feat_down, feat_line, feat_side_send, feat_side)
    me = lax.axis_index("atoms")
    group = lax.axis_index("waves")
    core = lax.rem(group, 2)
    partner = group + 1 - 2 * core
    half, channels = feat_ref.shape[1] * feat_ref.shape[2], feat_ref.shape[3]
    rows = 2 * half
    blocks_here = rows // BLOCK
    local_kernels = short_ref.shape[0]
    waves_each = wave_ref.shape[1] // 2
    part = mix_ref.shape[1] // (n // 2)
    per_tile = 128 // part

    lines = n // 2
    line, side = me // 2, lax.rem(me, 2)

    def peer(step):
        return lax.rem(me + step, n)

    def source(step):
        return lax.rem(me + n - step, n)

    def ranked(rank):
        closest = jnp.minimum(line, lines - 1 - line)
        away = (rank + 1) // 2
        near_line = jnp.where(lax.rem(rank, 2) == 1, line - away, line + away)
        far_line = jnp.where(line < lines - 1 - line, rank, lines - 1 - rank)
        return jnp.where(rank <= 2 * closest, near_line, far_line)

    def line_copy(sends, piece, slot, direction):
        up_send, down_send, line_recv, _, _ = sends
        return pltpu.make_async_remote_copy(
            src_ref=piece[0],
            dst_ref=piece[1],
            send_sem=(up_send if direction > 0 else down_send).at[slot],
            recv_sem=line_recv.at[slot],
            device_id={"atoms": me + 2 * direction},
            device_id_type=MESH,
        )

    def side_copy(sends, piece, slot):
        return pltpu.make_async_remote_copy(
            src_ref=piece[0],
            dst_ref=piece[1],
            send_sem=sends[3].at[slot],
            recv_sem=sends[4].at[slot],
            device_id={"atoms": me + 1 - 2 * side},
            device_id_type=MESH,
        )

    def feat_piece(shard_line, shard_side, which):
        place = feat_buf.at[2 * shard_line + shard_side, core, which]
        return place, place

    def send_own(sends, which):
        piece = (feat_ref.at[core, which], feat_buf.at[me, core, which])
        slot = line * PIECES + which

        @pl.when(line < lines - 1)
        def _():
            line_copy(sends, piece, slot, 1).start()

        @pl.when(line > 0)
        def _():
            line_copy(sends, piece, slot, -1).start()

        side_copy(sends, piece, slot).start()

    def pass_on(sends, shard_line, which):
        piece = feat_piece(shard_line, side, which)
        slot = shard_line * PIECES + which
        line_copy(sends, piece, slot, 1).wait_recv()

        @pl.when((shard_line < line) & (line < lines - 1))
        def _():
            line_copy(sends, piece, slot, 1).start()

        @pl.when((shard_line > line) & (line > 0))
        def _():
            line_copy(sends, piece, slot, -1).start()

        side_copy(sends, piece, slot).start()
        forward_copy(2 * shard_line + side, which).start()

    def finish(sends):
        def one(slot, carry):
            shard_line = slot // PIECES
            piece = feat_piece(shard_line, side, lax.rem(slot, PIECES))

            @pl.when((shard_line <= line) & (line < lines - 1))
            def _():
                line_copy(sends, piece, slot, 1).wait_send()

            @pl.when((shard_line >= line) & (line > 0))
            def _():
                line_copy(sends, piece, slot, -1).wait_send()

            side_copy(sends, piece, slot).wait_send()
            return carry

        lax.fori_loop(0, lines * PIECES, one, 0)

    def pos_copy(step):
        return pltpu.make_async_remote_copy(
            src_ref=pos_ref,
            dst_ref=pos_buf.at[me],
            send_sem=pos_send.at[step],
            recv_sem=pos_recv.at[step],
            device_id={"atoms": peer(step)},
            device_id_type=MESH,
        )

    def forward_copy(origin, which):
        return pltpu.make_async_remote_copy(
            src_ref=feat_buf.at[origin, core, which],
            dst_ref=feat_buf.at[origin, core, which],
            send_sem=fwd_send.at[origin * PIECES + which],
            recv_sem=fwd_recv.at[origin * PIECES + which],
            device_id={"waves": partner},
            device_id_type=MESH,
        )

    def sum_copy(step):
        return pltpu.make_async_remote_copy(
            src_ref=sum_send_buf.at[peer(step)],
            dst_ref=sum_buf.at[me],
            send_sem=sum_send.at[step],
            recv_sem=sum_recv.at[step],
            device_id={"atoms": peer(step)},
            device_id_type=MESH,
        )

    def msg_copy(step):
        target = lax.rem(group + step, groups)
        return pltpu.make_async_remote_copy(
            src_ref=send_buf.at[target],
            dst_ref=recv_buf.at[step],
            send_sem=msg_send.at[step],
            recv_sem=msg_recv.at[step],
            device_id={"waves": target},
            device_id_type=MESH,
        )

    own_feat = pltpu.make_async_copy(feat_ref, feat_buf.at[me], own_sem.at[0])
    own_pos = pltpu.make_async_copy(pos_ref, pos_buf.at[me], own_sem.at[1])
    loads = [
        pltpu.make_async_copy(held, kept, own_sem.at[2 + which])
        for which, (held, kept) in enumerate(
            (
                (wave_in, wave_ref),
                (mix_in, mix_ref),
                (latw_in, latw_ref),
                (rate_in, rate_ref),
                (short_in, short_ref),
                (outw_in, outw_ref),
            )
        )
    ]
    own_pos.start()
    for load in loads[:4]:
        load.start()
    own_feat.start()
    for load in loads[4:]:
        load.start()

    barrier = pltpu.get_barrier_semaphore()
    for step in range(1, n):
        pl.semaphore_signal(barrier, inc=1, device_id={"atoms": peer(step)}, device_id_type=MESH)
    for step in range(1, groups):
        pl.semaphore_signal(
            barrier,
            inc=1,
            device_id={"waves": lax.rem(group + step, groups)},
            device_id_type=MESH,
        )
    pl.semaphore_wait(barrier, n - 1 + groups - 1)

    for which in range(PIECES):
        send_own(feat_sends, which)
    for step in range(1, n):
        pos_copy(step).start()

    own_pos.wait()
    for load in loads[:4]:
        load.wait()
    tile = pl.ds(pl.multiple_of((line // per_tile) * 128, 128), 128)
    fused_w[...] = jnp.dot(
        latw_ref[...].astype(jnp.float32),
        mix_ref[:, tile],
        precision=lax.Precision.HIGHEST,
        preferred_element_type=jnp.float32,
    ).astype(jnp.bfloat16)
    spots = columns_of(pos_buf[me].astype(jnp.float32))

    begin = pl.multiple_of(side * waves_each, waves_each)
    own_waves = columns_of(wave_ref[:, pl.ds(begin, waves_each)].astype(jnp.float32))
    for axis in range(3):
        wave_cols[axis] = jnp.broadcast_to(own_waves[axis], (waves_each, 128))
    chunk = 64

    def phase_rows(origin, near):
        def some(which, carry):
            low = pl.multiple_of(which * chunk, chunk)
            waves = [wave_cols[axis, pl.ds(low, chunk), :] for axis in range(3)]
            for start in range(0, rows, 128):
                spot = [row[:, start : start + 128] for row in near]
                cosine, sine = cos_sin(turns(waves, spot))
                phase_buf[origin, pl.ds(low, chunk), start : start + 128] = cosine
                high = pl.multiple_of(waves_each + low, chunk)
                phase_buf[origin, pl.ds(high, chunk), start : start + 128] = sine
            return carry

        lax.fori_loop(0, waves_each // chunk, some, 0)

    factors[...] = jnp.zeros_like(factors)
    gathered[...] = jnp.zeros_like(gathered)
    own_feat.wait()
    norm_scale = 1.0 / math.sqrt(NBR * BLOCK)

    def use_shard(origin):
        feats = feat_buf[origin].reshape(rows, channels)
        near = rows_of(pos_buf[origin].astype(jnp.float32))
        latent = jnp.dot(feats, fused_w[...], preferred_element_type=jnp.float32)
        phase_rows(origin, near)
        factors[...] += jnp.dot(
            phase_buf[origin], latent.astype(jnp.bfloat16), preferred_element_type=jnp.float32
        )
        lane_block = lax.broadcasted_iota(jnp.int32, (1, rows), 1) // BLOCK
        for block in range(blocks_here):
            keep = jnp.zeros((1, rows), jnp.float32)
            for near_block in range(blocks_here):
                number = origin * blocks_here + near_block
                listed = jnp.float32(0.0)
                for slot in range(NBR):
                    listed += jnp.where(nbr_ref[block, slot] == number, norm_scale, 0.0)
                keep = keep + jnp.where(lane_block == near_block, listed, 0.0)
            low = block * BLOCK
            dist_sq = None
            for axis in range(3):
                gap = jnp.abs(spots[axis][low : low + BLOCK] - near[axis]) * (1.0 / 65536.0)
                gap = jnp.minimum(gap, 1.0 - gap)
                dist_sq = gap * gap if dist_sq is None else dist_sq + gap * gap
            distance = jnp.sqrt(dist_sq)
            smooth = jnp.maximum(1.0 - dist_sq * (1.0 / (cutoff * cutoff)), 0.0)
            smooth = smooth * smooth * keep
            for kernel in range(local_kernels):
                center = (group * local_kernels + kernel).astype(jnp.float32) * (
                    cutoff / (RADIAL - 1)
                )
                shaped = (distance - center) * (1.0 / width_ref[kernel])
                weights = (jnp.exp(-(shaped * shaped)) * smooth).astype(jnp.bfloat16)
                gathered[kernel, low : low + BLOCK, :] += jnp.dot(
                    weights, feats, preferred_element_type=jnp.float32
                )

    use_shard(me)

    def take(origin):
        pos_copy(lax.rem(me - origin + n, n)).wait_recv()
        for which in range(PIECES):
            forward_copy(origin, which).wait_recv()
        use_shard(origin)

    def gather_step(rank, carry):
        def stage(turn, inner):
            @pl.when(rank < lines)
            def _():
                for which in range(PIECES // 2):
                    pass_on(feat_sends, ranked(rank), turn * (PIECES // 2) + which)

            before = ranked(rank - 1)
            after = ranked(jnp.maximum(rank - 2, 0))

            @pl.when((turn == 1) & (rank <= lines))
            def _():
                for which in range(PIECES):
                    side_copy(
                        feat_sends,
                        feat_piece(before, 1 - side, which),
                        before * PIECES + which,
                    ).wait_recv()
                    forward_copy(2 * before + 1 - side, which).start()

            use_now = jnp.where(turn == 0, rank >= 2, (rank >= 2) & (rank <= lines))
            origin = jnp.where(turn == 0, 2 * after + 1 - side, 2 * before + side)

            @pl.when(use_now)
            def _():
                take(origin)

            return inner

        lax.fori_loop(0, jnp.where(rank <= lines, 2, 1), stage, 0)
        return carry

    lax.fori_loop(1, lines + 2, gather_step, 0)

    lengths = turns(own_waves, own_waves)
    gain = jnp.exp(-lengths * rate_ref[:, tile]) * (1.0 / math.sqrt(rows * n))
    filt_cols[...] = (factors[...] * jnp.concatenate([gain, gain], axis=0)).T
    turned = filt_cols[pl.ds(pl.multiple_of(lax.rem(line, per_tile) * part, part), part), :]
    filt_buf[...] = turned.astype(jnp.bfloat16)

    def sum_of(owner):
        sums = jnp.dot(filt_buf[...], phase_buf[owner], preferred_element_type=jnp.float32)
        return (sums * (1.0 / math.sqrt(K))).astype(jnp.bfloat16)

    def sum_step(step, carry):
        sum_send_buf[peer(step)] = sum_of(peer(step))
        sum_copy(step).start()
        return carry

    lax.fori_loop(1, n, sum_step, 0)
    sum_buf[me] = sum_of(me)
    for load in loads[4:]:
        load.wait()
    short = jnp.zeros(message.shape, jnp.float32)
    for kernel in range(local_kernels):
        short += jnp.dot(
            gathered[kernel].astype(jnp.bfloat16),
            short_ref[kernel],
            preferred_element_type=jnp.float32,
        )
    message[...] = short
    for step in range(1, n):
        sum_copy(step).wait_recv()
    for whole in range(lines):
        summed[whole * part : (whole + 1) * part, :] = sum_buf[2 * whole].astype(
            jnp.float32
        ) + sum_buf[2 * whole + 1].astype(jnp.float32)
    reduced = summed[...].T.astype(jnp.bfloat16)
    width = out_ref.shape[1]
    for target in range(groups):
        low = target * width
        part = message[:, low : low + width] + jnp.dot(
            reduced, outw_ref[:, low : low + width], preferred_element_type=jnp.float32
        )
        send_buf[target] = part.astype(jnp.bfloat16)
    for step in range(1, groups):
        msg_copy(step).start()
    total = send_buf[group].astype(jnp.float32)
    for step in range(1, groups):
        msg_copy(step).wait_recv()
        total += recv_buf[step].astype(jnp.float32)
    out_ref[...] = total.astype(out_ref.dtype)
    finish(feat_sends)

    def finish_step(step, carry):
        pos_copy(step).wait_send()
        sum_copy(step).wait_send()
        for which in range(PIECES):
            forward_copy(peer(step), which).wait_send()
        return carry

    lax.fori_loop(1, n, finish_step, 0)
    for step in range(1, groups):
        msg_copy(step).wait_send()


def fused(
    features,
    positions,
    neighbours,
    wavevectors,
    radial_width,
    short_weight,
    latent_weight,
    mix_weight,
    filter_rate,
    out_weight,
):
    n = lax.axis_size("atoms")
    groups = lax.axis_size("waves")
    rows, channels = features.shape
    latents = latent_weight.shape[1]
    waves_each = wavevectors.shape[1] // 2
    part = latents // (n // 2)
    local_kernels = radial_width.shape[0]
    vmem = pl.BlockSpec(memory_space=pltpu.VMEM)
    held = pl.BlockSpec(memory_space=pl.ANY)
    smem = pl.BlockSpec(memory_space=pltpu.SMEM)
    dma = pltpu.SemaphoreType.DMA
    return pl.pallas_call(
        functools.partial(fused_kernel, n, groups),
        out_shape=jax.ShapeDtypeStruct((rows, channels // groups), jnp.bfloat16),
        in_specs=[held, held, smem, held, smem, held, held, held, held, held],
        out_specs=vmem,
        scratch_shapes=[
            pltpu.VMEM(wavevectors.shape, jnp.int32),
            pltpu.VMEM(short_weight.shape, jnp.bfloat16),
            pltpu.VMEM(latent_weight.shape, jnp.bfloat16),
            pltpu.VMEM(mix_weight.shape, jnp.float32),
            pltpu.VMEM((1, latents), jnp.float32),
            pltpu.VMEM(out_weight.shape, jnp.bfloat16),
            pltpu.VMEM((n, 2, PIECES, rows // 2 // PIECES, channels), jnp.bfloat16),
            pltpu.VMEM((n, 3, rows), jnp.int32),
            pltpu.VMEM((channels, 128), jnp.bfloat16),
            pltpu.VMEM((2 * waves_each, 128), jnp.float32),
            pltpu.VMEM((local_kernels, rows, channels), jnp.float32),
            pltpu.VMEM((n, 2 * waves_each, rows), jnp.bfloat16),
            pltpu.VMEM((3, waves_each, 128), jnp.float32),
            pltpu.VMEM((128, 2 * waves_each), jnp.float32),
            pltpu.VMEM((part, 2 * waves_each), jnp.bfloat16),
            pltpu.VMEM((n, part, rows), jnp.bfloat16),
            pltpu.VMEM((n, part, rows), jnp.bfloat16),
            pltpu.VMEM((rows, channels), jnp.float32),
            pltpu.VMEM((latents, rows), jnp.float32),
            pltpu.VMEM((groups, rows, channels // groups), jnp.bfloat16),
            pltpu.VMEM((groups, rows, channels // groups), jnp.bfloat16),
            dma((8,)),
            *[dma((n // 2 * PIECES,)) for _ in range(5)],
            *[dma((n,)) for _ in range(2)],
            *[dma((n * PIECES,)) for _ in range(2)],
            *[dma((n,)) for _ in range(2)],
            *[dma((groups,)) for _ in range(2)],
        ],
        compiler_params=pltpu.CompilerParams(
            collective_id=0, has_side_effects=True, vmem_limit_bytes=67043328
        ),
    )(
        features.reshape(2, PIECES, rows // 2 // PIECES, channels),
        positions,
        neighbours,
        wavevectors,
        radial_width,
        short_weight,
        latent_weight,
        mix_weight,
        filter_rate.reshape(1, latents),
        out_weight,
    )


def layer(*arrays):
    features, wavevectors = arrays[0], arrays[3]
    n = lax.axis_size("atoms")
    groups = lax.axis_size("waves")
    rows = features.shape[0]
    reach_hops = -(-REACH // (rows // BLOCK))
    covers_all = 2 * reach_hops + 1 >= n
    if covers_all and groups % 2 == 0 and n % 2 == 0 and rows % (2 * BLOCK) == 0:
        lines = n // 2
        latents = arrays[6].shape[1]
        part = latents // lines
        if wavevectors.shape[1] % 256 == 0 and part in (32, 64, 128) and part * lines == latents:
            return fused(*arrays)
    return local(*arrays)


def solution(mesh):
    placed = (
        P("atoms", None),
        P(None, "atoms"),
        P("atoms", None),
        P(None, "waves"),
        P("waves"),
        P("waves", None, None),
        P(),
        P(),
        P(),
        P(),
    )
    return jax.shard_map(
        layer, mesh=mesh, in_specs=placed, out_specs=P("atoms", "waves"), check_vma=False
    )
```

```python
import functools
import math

import jax
import jax.numpy as jnp
from jax import lax
from jax.experimental import pallas as pl
from jax.experimental.pallas import tpu as pltpu
from jax.sharding import PartitionSpec as P

K = 4096
RADIAL = 8
BLOCK = 128
NBR = 12
REACH = 7


cutoff = 0.5


def shifted(value, axis, steps):
    count = lax.axis_size(axis)
    pairs = [(source, (source + steps) % count) for source in range(count)]
    return lax.ppermute(value, axis, pairs)


def kernels(own_pos, near_pos, centers, radial_width):
    offsets = own_pos[:, None, :, None] - near_pos[:, :, None, :]
    offsets = jnp.mod(offsets, 65536)
    offsets = jnp.where(offsets >= 32768, offsets - 65536, offsets)
    coords = offsets.astype(jnp.float32) * (1.0 / 65536.0)
    dist_sq = jnp.sum(coords * coords, axis=0)
    distance = jnp.sqrt(dist_sq)
    smooth = jnp.where(
        dist_sq < cutoff * cutoff, jnp.square(1.0 - dist_sq / (cutoff * cutoff)), 0.0
    )
    shaped = (distance[None] - centers[:, None, None, None]) / radial_width[:, None, None, None]
    norm_scale = 1.0 / math.sqrt(NBR * BLOCK)
    return (jnp.exp(-jnp.square(shaped)) * smooth[None] * norm_scale).astype(jnp.bfloat16)


def phases_of(wavevectors, spots):
    phase_turn = (
        wavevectors[0][:, None] * spots[0][None, :]
        + wavevectors[1][:, None] * spots[1][None, :]
        + wavevectors[2][:, None] * spots[2][None, :]
    )
    phase_turn = jnp.mod(phase_turn, 65536)
    angles = phase_turn.astype(jnp.float32) * (2.0 * math.pi / 65536.0)
    return jnp.concatenate([jnp.cos(angles), jnp.sin(angles)], axis=0).astype(jnp.bfloat16)


def filter_gain(wavevectors, filter_rate):
    lengths = jnp.sum(wavevectors * wavevectors, axis=0).astype(jnp.float32)
    return jnp.exp(-lengths[:, None] * filter_rate[None, :])


def local(
    features,
    positions,
    neighbours,
    wavevectors,
    radial_width,
    short_weight,
    latent_weight,
    mix_weight,
    filter_rate,
    out_weight,
):
    row_count = features.shape[0]
    channels = features.shape[1]
    blocks_here = row_count // BLOCK
    atom_devices = lax.axis_size("atoms")
    total_blocks = blocks_here * atom_devices
    reach_hops = -(-REACH // blocks_here)
    window_feat = []
    window_pos = []
    for offset in range(-reach_hops, reach_hops + 1):
        if offset == 0:
            arrived = (features, positions)
        else:
            arrived = shifted((features, positions), "atoms", -offset)
        window_feat.append(arrived[0])
        window_pos.append(arrived[1])
    window_feat = jnp.concatenate(window_feat, axis=0).reshape(-1, BLOCK, channels)
    window_pos = jnp.concatenate(window_pos, axis=1).reshape(3, -1, BLOCK)
    first_block = lax.axis_index("atoms") * blocks_here - reach_hops * blocks_here
    local_near = jnp.mod(neighbours - first_block, total_blocks)
    own_pos = positions.reshape(3, blocks_here, BLOCK)
    local_kernels = radial_width.shape[0]
    kernel_ids = lax.axis_index("waves") * local_kernels + jnp.arange(
        local_kernels, dtype=jnp.int32
    )
    centers = cutoff * kernel_ids.astype(jnp.float32) / (RADIAL - 1)
    flat_weight = short_weight.reshape(local_kernels * channels, channels)

    def short_block(block_index):
        near_blocks = local_near[block_index]
        near_feat = window_feat[near_blocks]
        near_pos = window_pos[:, near_blocks]
        weights = kernels(own_pos[:, block_index], near_pos, centers, radial_width)
        gathered = jnp.einsum(
            "rjia,jac->irc", weights, near_feat, preferred_element_type=jnp.float32
        )
        gathered = gathered.astype(jnp.bfloat16).reshape(BLOCK, local_kernels * channels)
        return jnp.dot(gathered, flat_weight, preferred_element_type=jnp.float32)

    short_range = lax.map(short_block, jnp.arange(blocks_here, dtype=jnp.int32)).reshape(
        row_count, channels
    )
    latent = jnp.dot(features, latent_weight, preferred_element_type=jnp.float32).astype(
        jnp.bfloat16
    )
    phases = phases_of(wavevectors, positions)
    partial_factors = jnp.dot(phases, latent, preferred_element_type=jnp.float32)
    gain = filter_gain(wavevectors, filter_rate)
    gain = jnp.concatenate([gain, gain], axis=0)
    norm_scale = 1.0 / math.sqrt(row_count * atom_devices)
    factors = lax.psum(partial_factors, "atoms")
    mixed = jnp.dot(factors, mix_weight, precision=lax.Precision.HIGHEST)
    filtered = (gain * mixed * norm_scale).astype(jnp.bfloat16)
    summed = lax.dot_general(
        phases, filtered, (((0,), (0,)), ((), ())), preferred_element_type=jnp.float32
    )
    summed = (summed * (1.0 / math.sqrt(K))).astype(jnp.bfloat16)
    long_range = jnp.dot(summed, out_weight, preferred_element_type=jnp.float32)
    combined = lax.psum_scatter(
        (short_range + long_range).astype(jnp.bfloat16), "waves", scatter_dimension=1, tiled=True
    )
    return combined


MESH = pl.DeviceIdType.MESH
PIECES = 4
SINE = (6.28318516, -41.34165503, 81.60100405, -76.5497817, 39.53670129)


def sine_of_turn(quarter):
    square = quarter * quarter
    total = SINE[-1] * square + SINE[-2]
    for factor in SINE[-3::-1]:
        total = total * square + factor
    return total * quarter


def cos_sin(turn):
    turn = turn * (1.0 / 65536.0)
    turn = turn - jnp.floor(turn + 0.5)
    shifted_turn = turn - 0.25
    shifted_turn = jnp.where(shifted_turn < -0.5, shifted_turn + 1.0, shifted_turn)
    return (
        sine_of_turn(0.25 - jnp.abs(turn)).astype(jnp.bfloat16),
        sine_of_turn(0.25 - jnp.abs(shifted_turn)).astype(jnp.bfloat16),
    )


def columns_of(rows):
    padded = jnp.concatenate([rows, jnp.zeros((5, rows.shape[1]), jnp.float32)], axis=0)
    turned = padded.T
    return [turned[:, axis : axis + 1] for axis in range(3)]


def rows_of(rows):
    return [rows[axis : axis + 1, :] for axis in range(3)]


def turns(first, second):
    return first[0] * second[0] + first[1] * second[1] + first[2] * second[2]


def fused_kernel(
    n,
    groups,
    feat_ref,
    pos_ref,
    nbr_ref,
    wave_in,
    width_ref,
    short_in,
    latw_in,
    mix_in,
    rate_in,
    outw_in,
    out_ref,
    wave_ref,
    short_ref,
    latw_ref,
    mix_ref,
    rate_ref,
    outw_ref,
    feat_buf,
    pos_buf,
    fused_w,
    factors,
    gathered,
    phase_buf,
    wave_cols,
    filt_cols,
    filt_buf,
    sum_send_buf,
    sum_buf,
    message,
    summed,
    send_buf,
    recv_buf,
    own_sem,
    feat_up,
    feat_down,
    feat_line,
    feat_side_send,
    feat_side,
    pos_send,
    pos_recv,
    fwd_send,
    fwd_recv,
    sum_send,
    sum_recv,
    msg_send,
    msg_recv,
):
    feat_sends = (feat_up, feat_down, feat_line, feat_side_send, feat_side)
    me = lax.axis_index("atoms")
    group = lax.axis_index("waves")
    core = lax.rem(group, 2)
    partner = group + 1 - 2 * core
    half, channels = feat_ref.shape[1] * feat_ref.shape[2], feat_ref.shape[3]
    rows = 2 * half
    blocks_here = rows // BLOCK
    local_kernels = short_ref.shape[0]
    waves_each = wave_ref.shape[1] // 2
    part = mix_ref.shape[1] // (n // 2)
    per_tile = 128 // part

    lines = n // 2
    line, side = me // 2, lax.rem(me, 2)

    def peer(step):
        return lax.rem(me + step, n)

    def source(step):
        return lax.rem(me + n - step, n)

    def ranked(rank):
        closest = jnp.minimum(line, lines - 1 - line)
        away = (rank + 1) // 2
        near_line = jnp.where(lax.rem(rank, 2) == 1, line - away, line + away)
        far_line = jnp.where(line < lines - 1 - line, rank, lines - 1 - rank)
        return jnp.where(rank <= 2 * closest, near_line, far_line)

    def line_copy(sends, piece, slot, direction):
        up_send, down_send, line_recv, _, _ = sends
        return pltpu.make_async_remote_copy(
            src_ref=piece[0],
            dst_ref=piece[1],
            send_sem=(up_send if direction > 0 else down_send).at[slot],
            recv_sem=line_recv.at[slot],
            device_id={"atoms": me + 2 * direction},
            device_id_type=MESH,
        )

    def side_copy(sends, piece, slot):
        return pltpu.make_async_remote_copy(
            src_ref=piece[0],
            dst_ref=piece[1],
            send_sem=sends[3].at[slot],
            recv_sem=sends[4].at[slot],
            device_id={"atoms": me + 1 - 2 * side},
            device_id_type=MESH,
        )

    def feat_piece(shard_line, shard_side, which):
        place = feat_buf.at[2 * shard_line + shard_side, core, which]
        return place, place

    def send_own(sends, which):
        piece = (feat_ref.at[core, which], feat_buf.at[me, core, which])
        slot = line * PIECES + which

        @pl.when(line < lines - 1)
        def _():
            line_copy(sends, piece, slot, 1).start()

        @pl.when(line > 0)
        def _():
            line_copy(sends, piece, slot, -1).start()

        side_copy(sends, piece, slot).start()

    def pass_on(sends, shard_line, which):
        piece = feat_piece(shard_line, side, which)
        slot = shard_line * PIECES + which
        line_copy(sends, piece, slot, 1).wait_recv()

        @pl.when((shard_line < line) & (line < lines - 1))
        def _():
            line_copy(sends, piece, slot, 1).start()

        @pl.when((shard_line > line) & (line > 0))
        def _():
            line_copy(sends, piece, slot, -1).start()

        side_copy(sends, piece, slot).start()
        forward_copy(2 * shard_line + side, which).start()

    def finish(sends):
        def one(slot, carry):
            shard_line = slot // PIECES
            piece = feat_piece(shard_line, side, lax.rem(slot, PIECES))

            @pl.when((shard_line <= line) & (line < lines - 1))
            def _():
                line_copy(sends, piece, slot, 1).wait_send()

            @pl.when((shard_line >= line) & (line > 0))
            def _():
                line_copy(sends, piece, slot, -1).wait_send()

            side_copy(sends, piece, slot).wait_send()
            return carry

        lax.fori_loop(0, lines * PIECES, one, 0)

    def pos_copy(step):
        return pltpu.make_async_remote_copy(
            src_ref=pos_ref,
            dst_ref=pos_buf.at[me],
            send_sem=pos_send.at[step],
            recv_sem=pos_recv.at[step],
            device_id={"atoms": peer(step)},
            device_id_type=MESH,
        )

    def forward_copy(origin, which):
        return pltpu.make_async_remote_copy(
            src_ref=feat_buf.at[origin, core, which],
            dst_ref=feat_buf.at[origin, core, which],
            send_sem=fwd_send.at[origin * PIECES + which],
            recv_sem=fwd_recv.at[origin * PIECES + which],
            device_id={"waves": partner},
            device_id_type=MESH,
        )

    def sum_copy(step):
        return pltpu.make_async_remote_copy(
            src_ref=sum_send_buf.at[peer(step)],
            dst_ref=sum_buf.at[me],
            send_sem=sum_send.at[step],
            recv_sem=sum_recv.at[step],
            device_id={"atoms": peer(step)},
            device_id_type=MESH,
        )

    def msg_copy(step):
        target = lax.rem(group + step, groups)
        return pltpu.make_async_remote_copy(
            src_ref=send_buf.at[target],
            dst_ref=recv_buf.at[step],
            send_sem=msg_send.at[step],
            recv_sem=msg_recv.at[step],
            device_id={"waves": target},
            device_id_type=MESH,
        )

    own_feat = pltpu.make_async_copy(feat_ref, feat_buf.at[me], own_sem.at[0])
    own_pos = pltpu.make_async_copy(pos_ref, pos_buf.at[me], own_sem.at[1])
    loads = [
        pltpu.make_async_copy(held, kept, own_sem.at[2 + which])
        for which, (held, kept) in enumerate(
            (
                (wave_in, wave_ref),
                (mix_in, mix_ref),
                (latw_in, latw_ref),
                (rate_in, rate_ref),
                (short_in, short_ref),
                (outw_in, outw_ref),
            )
        )
    ]
    own_pos.start()
    for load in loads[:4]:
        load.start()
    own_feat.start()
    for load in loads[4:]:
        load.start()

    barrier = pltpu.get_barrier_semaphore()
    for step in range(1, n):
        pl.semaphore_signal(barrier, inc=1, device_id={"atoms": peer(step)}, device_id_type=MESH)
    for step in range(1, groups):
        pl.semaphore_signal(
            barrier,
            inc=1,
            device_id={"waves": lax.rem(group + step, groups)},
            device_id_type=MESH,
        )
    pl.semaphore_wait(barrier, n - 1 + groups - 1)

    for which in range(PIECES):
        send_own(feat_sends, which)
    for step in range(1, n):
        pos_copy(step).start()

    own_pos.wait()
    for load in loads[:4]:
        load.wait()
    tile = pl.ds(pl.multiple_of((line // per_tile) * 128, 128), 128)
    fused_w[...] = jnp.dot(
        latw_ref[...].astype(jnp.float32),
        mix_ref[:, tile],
        precision=lax.Precision.HIGHEST,
        preferred_element_type=jnp.float32,
    ).astype(jnp.bfloat16)
    spots = columns_of(pos_buf[me].astype(jnp.float32))

    begin = pl.multiple_of(side * waves_each, waves_each)
    own_waves = columns_of(wave_ref[:, pl.ds(begin, waves_each)].astype(jnp.float32))
    for axis in range(3):
        wave_cols[axis] = jnp.broadcast_to(own_waves[axis], (waves_each, 128))
    chunk = 64

    def phase_rows(origin, near):
        def some(which, carry):
            low = pl.multiple_of(which * chunk, chunk)
            waves = [wave_cols[axis, pl.ds(low, chunk), :] for axis in range(3)]
            for start in range(0, rows, 128):
                spot = [row[:, start : start + 128] for row in near]
                cosine, sine = cos_sin(turns(waves, spot))
                phase_buf[origin, pl.ds(low, chunk), start : start + 128] = cosine
                high = pl.multiple_of(waves_each + low, chunk)
                phase_buf[origin, pl.ds(high, chunk), start : start + 128] = sine
            return carry

        lax.fori_loop(0, waves_each // chunk, some, 0)

    factors[...] = jnp.zeros_like(factors)
    gathered[...] = jnp.zeros_like(gathered)
    own_feat.wait()
    norm_scale = 1.0 / math.sqrt(NBR * BLOCK)

    def use_shard(origin):
        feats = feat_buf[origin].reshape(rows, channels)
        near = rows_of(pos_buf[origin].astype(jnp.float32))
        latent = jnp.dot(feats, fused_w[...], preferred_element_type=jnp.float32)
        phase_rows(origin, near)
        factors[...] += jnp.dot(
            phase_buf[origin], latent.astype(jnp.bfloat16), preferred_element_type=jnp.float32
        )
        lane_block = lax.broadcasted_iota(jnp.int32, (1, rows), 1) // BLOCK
        for block in range(blocks_here):
            keep = jnp.zeros((1, rows), jnp.float32)
            for near_block in range(blocks_here):
                number = origin * blocks_here + near_block
                listed = jnp.float32(0.0)
                for slot in range(NBR):
                    listed += jnp.where(nbr_ref[block, slot] == number, norm_scale, 0.0)
                keep = keep + jnp.where(lane_block == near_block, listed, 0.0)
            low = block * BLOCK
            dist_sq = None
            for axis in range(3):
                gap = jnp.abs(spots[axis][low : low + BLOCK] - near[axis]) * (1.0 / 65536.0)
                gap = jnp.minimum(gap, 1.0 - gap)
                dist_sq = gap * gap if dist_sq is None else dist_sq + gap * gap
            distance = jnp.sqrt(dist_sq)
            smooth = jnp.maximum(1.0 - dist_sq * (1.0 / (cutoff * cutoff)), 0.0)
            smooth = smooth * smooth * keep
            for kernel in range(local_kernels):
                center = (group * local_kernels + kernel).astype(jnp.float32) * (
                    cutoff / (RADIAL - 1)
                )
                shaped = (distance - center) * (1.0 / width_ref[kernel])
                weights = (jnp.exp(-(shaped * shaped)) * smooth).astype(jnp.bfloat16)
                gathered[kernel, low : low + BLOCK, :] += jnp.dot(
                    weights, feats, preferred_element_type=jnp.float32
                )

    use_shard(me)

    def take(origin):
        pos_copy(lax.rem(me - origin + n, n)).wait_recv()
        for which in range(PIECES):
            forward_copy(origin, which).wait_recv()
        use_shard(origin)

    def gather_step(rank, carry):
        def stage(turn, inner):
            @pl.when(rank < lines)
            def _():
                for which in range(PIECES // 2):
                    pass_on(feat_sends, ranked(rank), turn * (PIECES // 2) + which)

            before = ranked(rank - 1)
            after = ranked(jnp.maximum(rank - 2, 0))

            @pl.when((turn == 1) & (rank <= lines))
            def _():
                for which in range(PIECES):
                    side_copy(
                        feat_sends,
                        feat_piece(before, 1 - side, which),
                        before * PIECES + which,
                    ).wait_recv()
                    forward_copy(2 * before + 1 - side, which).start()

            use_now = jnp.where(turn == 0, rank >= 2, (rank >= 2) & (rank <= lines))
            origin = jnp.where(turn == 0, 2 * after + 1 - side, 2 * before + side)

            @pl.when(use_now)
            def _():
                take(origin)

            return inner

        lax.fori_loop(0, jnp.where(rank <= lines, 2, 1), stage, 0)
        return carry

    lax.fori_loop(1, lines + 2, gather_step, 0)

    lengths = turns(own_waves, own_waves)
    gain = jnp.exp(-lengths * rate_ref[:, tile]) * (1.0 / math.sqrt(rows * n))
    filt_cols[...] = (factors[...] * jnp.concatenate([gain, gain], axis=0)).T
    turned = filt_cols[pl.ds(pl.multiple_of(lax.rem(line, per_tile) * part, part), part), :]
    filt_buf[...] = turned.astype(jnp.bfloat16)

    def sum_of(owner):
        sums = jnp.dot(filt_buf[...], phase_buf[owner], preferred_element_type=jnp.float32)
        return (sums * (1.0 / math.sqrt(K))).astype(jnp.bfloat16)

    def sum_step(step, carry):
        sum_send_buf[peer(step)] = sum_of(peer(step))
        sum_copy(step).start()
        return carry

    lax.fori_loop(1, n, sum_step, 0)
    sum_buf[me] = sum_of(me)
    for load in loads[4:]:
        load.wait()
    short = jnp.zeros(message.shape, jnp.float32)
    for kernel in range(local_kernels):
        short += jnp.dot(
            gathered[kernel].astype(jnp.bfloat16),
            short_ref[kernel],
            preferred_element_type=jnp.float32,
        )
    message[...] = short
    for step in range(1, n):
        sum_copy(step).wait_recv()
    for whole in range(lines):
        summed[whole * part : (whole + 1) * part, :] = sum_buf[2 * whole].astype(
            jnp.float32
        ) + sum_buf[2 * whole + 1].astype(jnp.float32)
    reduced = summed[...].T.astype(jnp.bfloat16)
    width = out_ref.shape[1]
    order = sorted(range(1, groups), key=lambda step: abs(step - groups // 2))
    for step in [*order, 0]:
        target = lax.rem(group + step, groups)
        columns = pl.ds(pl.multiple_of(target * width, width), width)
        part_sum = message[:, columns] + jnp.dot(
            reduced, outw_ref[:, columns], preferred_element_type=jnp.float32
        )
        if step == 0:
            total = part_sum
        else:
            send_buf[target] = part_sum.astype(jnp.bfloat16)
            msg_copy(step).start()
    for step in range(1, groups):
        msg_copy(step).wait_recv()
        total += recv_buf[step].astype(jnp.float32)
    out_ref[...] = total.astype(out_ref.dtype)
    finish(feat_sends)

    def finish_step(step, carry):
        pos_copy(step).wait_send()
        sum_copy(step).wait_send()
        for which in range(PIECES):
            forward_copy(peer(step), which).wait_send()
        return carry

    lax.fori_loop(1, n, finish_step, 0)
    for step in range(1, groups):
        msg_copy(step).wait_send()


def fused(
    features,
    positions,
    neighbours,
    wavevectors,
    radial_width,
    short_weight,
    latent_weight,
    mix_weight,
    filter_rate,
    out_weight,
):
    n = lax.axis_size("atoms")
    groups = lax.axis_size("waves")
    rows, channels = features.shape
    latents = latent_weight.shape[1]
    waves_each = wavevectors.shape[1] // 2
    part = latents // (n // 2)
    local_kernels = radial_width.shape[0]
    vmem = pl.BlockSpec(memory_space=pltpu.VMEM)
    held = pl.BlockSpec(memory_space=pl.ANY)
    smem = pl.BlockSpec(memory_space=pltpu.SMEM)
    dma = pltpu.SemaphoreType.DMA
    return pl.pallas_call(
        functools.partial(fused_kernel, n, groups),
        out_shape=jax.ShapeDtypeStruct((rows, channels // groups), jnp.bfloat16),
        in_specs=[held, held, smem, held, smem, held, held, held, held, held],
        out_specs=vmem,
        scratch_shapes=[
            pltpu.VMEM(wavevectors.shape, jnp.int32),
            pltpu.VMEM(short_weight.shape, jnp.bfloat16),
            pltpu.VMEM(latent_weight.shape, jnp.bfloat16),
            pltpu.VMEM(mix_weight.shape, jnp.float32),
            pltpu.VMEM((1, latents), jnp.float32),
            pltpu.VMEM(out_weight.shape, jnp.bfloat16),
            pltpu.VMEM((n, 2, PIECES, rows // 2 // PIECES, channels), jnp.bfloat16),
            pltpu.VMEM((n, 3, rows), jnp.int32),
            pltpu.VMEM((channels, 128), jnp.bfloat16),
            pltpu.VMEM((2 * waves_each, 128), jnp.float32),
            pltpu.VMEM((local_kernels, rows, channels), jnp.float32),
            pltpu.VMEM((n, 2 * waves_each, rows), jnp.bfloat16),
            pltpu.VMEM((3, waves_each, 128), jnp.float32),
            pltpu.VMEM((128, 2 * waves_each), jnp.float32),
            pltpu.VMEM((part, 2 * waves_each), jnp.bfloat16),
            pltpu.VMEM((n, part, rows), jnp.bfloat16),
            pltpu.VMEM((n, part, rows), jnp.bfloat16),
            pltpu.VMEM((rows, channels), jnp.float32),
            pltpu.VMEM((latents, rows), jnp.float32),
            pltpu.VMEM((groups, rows, channels // groups), jnp.bfloat16),
            pltpu.VMEM((groups, rows, channels // groups), jnp.bfloat16),
            dma((8,)),
            *[dma((n // 2 * PIECES,)) for _ in range(5)],
            *[dma((n,)) for _ in range(2)],
            *[dma((n * PIECES,)) for _ in range(2)],
            *[dma((n,)) for _ in range(2)],
            *[dma((groups,)) for _ in range(2)],
        ],
        compiler_params=pltpu.CompilerParams(
            collective_id=0, has_side_effects=True, vmem_limit_bytes=67043328
        ),
    )(
        features.reshape(2, PIECES, rows // 2 // PIECES, channels),
        positions,
        neighbours,
        wavevectors,
        radial_width,
        short_weight,
        latent_weight,
        mix_weight,
        filter_rate.reshape(1, latents),
        out_weight,
    )


def layer(*arrays):
    features, wavevectors = arrays[0], arrays[3]
    n = lax.axis_size("atoms")
    groups = lax.axis_size("waves")
    rows = features.shape[0]
    reach_hops = -(-REACH // (rows // BLOCK))
    covers_all = 2 * reach_hops + 1 >= n
    if covers_all and groups % 2 == 0 and n % 2 == 0 and rows % (2 * BLOCK) == 0:
        lines = n // 2
        latents = arrays[6].shape[1]
        part = latents // lines
        if wavevectors.shape[1] % 256 == 0 and part in (32, 64, 128) and part * lines == latents:
            return fused(*arrays)
    return local(*arrays)


def solution(mesh):
    placed = (
        P("atoms", None),
        P(None, "atoms"),
        P("atoms", None),
        P(None, "waves"),
        P("waves"),
        P("waves", None, None),
        P(),
        P(),
        P(),
        P(),
    )
    return jax.shard_map(
        layer, mesh=mesh, in_specs=placed, out_specs=P("atoms", "waves"), check_vma=False
    )
```
